32 devices in a mesh: seq: 4 (over y, x), fsdp: 8 (over z, core).
Axes of the slice: x: 2, y: 2, z: 4, core: 2. Of those that a mesh axis runs over, the one named last changes fastest.
Arguments:
- tokens: bfloat16 [8, 1024, 768], P('fsdp', 'seq'), may hold values from -6 to 6
- cotangent: bfloat16 [8, 1024, 768], P('fsdp', 'seq'), may hold values from -6 to 6
- w_qkv: bfloat16 [768, 2304], P('fsdp'), may hold values from -0.21875 to 0.21875
- w_out: bfloat16 [768, 768], P('fsdp'), may hold values from -3.5 to 3.5
- w_gate: bfloat16 [768, 3072], P('fsdp'), may hold values from -0.21875 to 0.21875
- w_up: bfloat16 [768, 3072], P('fsdp'), may hold values from -0.21875 to 0.21875
- w_down: bfloat16 [3072, 768], P('fsdp'), may hold values from -0.21875 to 0.21875
- gain_one: bfloat16 [768], P('fsdp'), may hold values from 0.5 to 1.5
- bias_one: bfloat16 [768], P('fsdp'), may hold values from -1 to 1
- gain_two: bfloat16 [768], P('fsdp'), may hold values from 0.5 to 1.5
- bias_two: bfloat16 [768], P('fsdp'), may hold values from -1 to 1
- seq_lens: int32 [8], replicated, may hold values from 256 to 1024, as said below
- slot_seq: int32 [8], replicated, may hold values from 0 to 7, each once
Outputs:
- layer_out: bfloat16 [8, 1024, 768], P('fsdp', 'seq')
- grad_tokens: bfloat16 [8, 1024, 768], P('fsdp', 'seq')
- grad_qkv: float32 [768, 2304], P('fsdp')
- grad_out: float32 [768, 768], P('fsdp')
- grad_gate: float32 [768, 3072], P('fsdp')
- grad_up: float32 [768, 3072], P('fsdp')
- grad_down: float32 [3072, 768], P('fsdp')
- grad_gain_one: float32 [768], P('fsdp')
- grad_bias_one: float32 [768], P('fsdp')
- grad_gain_two: float32 [768], P('fsdp')
- grad_bias_two: float32 [768], P('fsdp')
- stream_rms: float32 [3], replicated
The draws below stay inside these ranges and needn't reach their ends.
Inputs may be any that keep to these rules, and one draw needn't show every extreme that they name: `seq_lens`: one sequence has 1024 valid tokens and one has 256. `slot_seq`: each sequence is held by exactly one slot.
All inputs are finite; a program needn't handle non-finite values.
Results may differ from the reference program's by a relative error of at most 0.02.
Values may be sent and summed in bfloat16 or wider, within the bound.
No kernel may reach another device: no remote copies, remote signals or barrier semaphores. Data moves between devices by JAX's collectives and lax.ppermute only.
A program may use at most 128 MiB of HBM per device.

```python
import jax
import jax.numpy as jnp
from jax import lax

D = 768
H = 12
HD = 64
FF = 3072
SEQLEN = 1024
SLOTS = 8


def draw_seq_lens(key, part):
    first_key, second_key = jax.random.split(jax.random.fold_in(key, 11))
    lengths = jax.random.randint(first_key, (SLOTS,), SEQLEN // 4, SEQLEN + 1, dtype=jnp.int32)
    order = jax.random.permutation(second_key, SLOTS)
    lengths = lengths.at[order[0]].set(SEQLEN)
    return lengths.at[order[1]].set(SEQLEN // 4)


def spiked(array, key, source, target, blocks, factor):
    owner, partner = [(jnp.arange(array.shape[axis_at]) // (array.shape[axis_at] // blocks)).reshape([-1 if axis == axis_at else 1 for axis in range(array.ndim)]) for axis_at in (source, target)]
    chosen = jax.random.permutation(key, blocks)[partner]
    strong = (owner == chosen) | (owner == (partner + blocks // 2) % blocks)
    return jnp.where(strong, factor * array, array)


def level_of(key, shape, pieces, low, top_value):
    factor_of = 1.0
    for axis_at, parts in pieces:
        steps = jax.random.uniform(jax.random.fold_in(jax.random.fold_in(key, 6), axis_at), (parts,), jnp.float32, low / len(pieces), top_value / len(pieces))
        factor_of = factor_of * jnp.repeat(jnp.exp(steps), shape[axis_at] // parts).reshape((-1,) + (1,) * (len(shape) - 1 - axis_at))
    return factor_of


def normal_values(rng, shape, width, bound, cuts=(), kind=jnp.bfloat16):
    level = level_of(rng, shape, cuts, -0.22, 0.18) if cuts else 1.0
    drawn = jax.random.normal(rng, shape, jnp.float32) * width * level
    return jnp.minimum(jnp.maximum(drawn, -bound), bound).astype(kind)


def bell_draw_with(key, dims, deviation, reach, cuts, heavy, kind=jnp.bfloat16):
    drawn = deviation * jax.random.normal(key, dims, jnp.float32)
    if cuts:
        drawn = drawn * level_of(key, dims, cuts, -0.22, 0.18)
    return jnp.clip(spiked(drawn, jax.random.fold_in(key, 3), *heavy), -reach, reach).astype(kind)


def setup_inputs(seed: int = 0) -> dict:
    splits = jax.random.split(jax.random.key(seed), 14)
    tokens = bell_draw_with(splits[0], (SLOTS, SEQLEN, D), 1.0, 6.0, ((0, 8), (1, 4)), (0, 2, 8, 2.0))
    cotangent = bell_draw_with(splits[1], (SLOTS, SEQLEN, D), 1.0, 6.0, ((0, 8), (1, 4)), (0, 2, 8, 2.0))
    w_qkv = normal_values(splits[2], (D, 3 * D), D ** -0.5, 0.21875, ((0, 8),))
    w_out = normal_values(splits[3], (D, D), (max(1, 4 * D // SEQLEN)) ** -0.5, 3.5, ((0, 8),))
    w_gate = normal_values(splits[4], (D, FF), D ** -0.5, 0.21875, ((0, 8),))
    w_up = normal_values(splits[5], (D, FF), D ** -0.5, 0.21875, ((0, 8),))
    w_down = normal_values(splits[6], (FF, D), (FF // 4) ** -0.5, 0.21875, ((0, 8),))
    gain_one = jnp.clip(1.0 + 0.1 * jax.random.normal(splits[7], (D,), jnp.float32), 0.5, 1.5).astype(jnp.bfloat16)
    bias_one = normal_values(splits[8], (D,), 0.2, 1.0, ((0, 8),))
    gain_two = jnp.clip(1.0 + 0.1 * jax.random.normal(splits[9], (D,), jnp.float32), 0.5, 1.5).astype(jnp.bfloat16)
    bias_two = normal_values(splits[10], (D,), 0.2, 1.0, ((0, 8),))
    seq_lens = draw_seq_lens(jax.random.fold_in(splits[13], 71), 0)
    slot_seq = jax.random.permutation(splits[12], SLOTS).astype(jnp.int32)
    return dict(tokens=tokens, cotangent=cotangent, w_qkv=w_qkv, w_out=w_out, w_gate=w_gate, w_up=w_up, w_down=w_down, gain_one=gain_one, bias_one=bias_one, gain_two=gain_two, bias_two=bias_two, seq_lens=seq_lens, slot_seq=slot_seq)


epsilon = 1e-12
rope_base = 1000.0
highest = lax.Precision.HIGHEST

@jax.custom_vjp
def low(v):
    return lax.optimization_barrier(v.astype(jnp.bfloat16)).astype(jnp.float32)

@jax.custom_vjp
def low_back(v):
    return v

def low_keep(v):
    return (low(v), None)

def low_pass(kept, grad):
    return (grad,)

def back_keep(v):
    return (v, None)

def back_low(kept, grad):
    return (low(grad),)
low.defvjp(low_keep, low_pass)
low_back.defvjp(back_keep, back_low)

def matmul(left_side, right_side):
    return jnp.dot(left_side, right_side, precision=highest, preferred_element_type=jnp.float32)

def rope_tables(positions, head_size):
    half_size = head_size // 2
    exponent = jnp.arange(half_size, dtype=jnp.float32) * (2.0 / head_size)
    frequency = jnp.power(jnp.float32(rope_base), -exponent)
    angles = positions[:, None] * frequency[None, :]
    cos_half = jnp.cos(angles)
    sin_half = jnp.sin(angles)
    return (jnp.concatenate([cos_half, cos_half], axis=-1), jnp.concatenate([sin_half, sin_half], axis=-1))

def rotate(values_in, cos_table, sin_table):
    half_size = values_in.shape[-1] // 2
    turned = jnp.concatenate([-values_in[..., half_size:], values_in[..., :half_size]], axis=-1)
    return values_in * cos_table + turned * sin_table

def layer_norm(stream, gain_vec, bias_vec):
    average = lax.optimization_barrier(jnp.mean(stream, axis=-1, keepdims=True))
    centred = stream - average
    variance = lax.optimization_barrier(jnp.mean(centred * centred, axis=-1, keepdims=True))
    return centred * lax.rsqrt(variance + epsilon) * gain_vec + bias_vec

def slot_layer(stream, weights, keep_mask, cos_table, sin_table):
    w_qkv, w_out, w_gate, w_up, w_down, gain_one, bias_one, gain_two, bias_two = weights
    length = stream.shape[0]
    projected = low_back(matmul(stream, w_qkv)).reshape(length, 3, H, HD)
    cos_wide = cos_table[:, None, :]
    sin_wide = sin_table[:, None, :]
    queries = low_back(low(rotate(projected[:, 0], cos_wide, sin_wide)))
    key_rows = low_back(low(rotate(projected[:, 1], cos_wide, sin_wide)))
    values = low_back(low(projected[:, 2]))
    scores = jnp.einsum('qhe,khe->hqk', queries, key_rows, precision=highest) * HD ** (-0.5)
    scores = low_back(scores)
    scores = jnp.where(keep_mask[None, None, :] > 0.5, scores, -1e+30)
    attn_probs = low(jax.nn.softmax(scores, axis=-1))
    attended = jnp.einsum('hqk,khe->qhe', attn_probs, values, precision=highest)
    head_mix = low_back(low(attended.reshape(length, D)))
    branch_attn = low_back(matmul(head_mix, w_out))
    normed_one = low(layer_norm(stream + branch_attn, gain_one, bias_one))
    gate_proj = low_back(matmul(normed_one, w_gate))
    up_proj = low_back(matmul(normed_one, w_up))
    inner_act = low(jax.nn.silu(gate_proj) * up_proj)
    branch_ffn = low_back(matmul(inner_act, w_down))
    result = layer_norm(normed_one + branch_ffn, gain_two, bias_two) * keep_mask[:, None]
    return (result, (branch_attn, branch_ffn))

def add_arrays(left_side, right_side):
    return left_side + right_side

def reference(tokens, cotangent, w_qkv, w_out, w_gate, w_up, w_down, gain_one, bias_one, gain_two, bias_two, seq_lens, slot_seq):
    weights = tuple((weight.astype(jnp.float32) for weight in (w_qkv, w_out, w_gate, w_up, w_down, gain_one, bias_one, gain_two, bias_two)))
    length = tokens.shape[1]
    cos_table, sin_table = rope_tables(jnp.arange(length, dtype=jnp.float32), HD)
    slot_lengths = seq_lens[slot_seq]
    keep_all = (jnp.arange(length, dtype=jnp.int32)[None, :] < slot_lengths[:, None]).astype(jnp.float32)

    def one_slot(state_sum, slot_data):
        gradients, square_sum = state_sum
        stream, grad_rows, keep_mask = slot_data

        def forward(stream_in, params):
            return slot_layer(stream_in, params, keep_mask, cos_table, sin_table)
        result, pull_back, branches = jax.vjp(forward, stream, weights, has_aux=True)
        grad_stream, grad_weights = pull_back(grad_rows)
        branch_attn, branch_ffn = branches
        column = keep_mask[:, None]
        squares = jnp.stack([jnp.sum(column * stream * stream), jnp.sum(column * branch_attn * branch_attn), jnp.sum(column * branch_ffn * branch_ffn)])
        gradients = jax.tree.map(add_arrays, gradients, grad_weights)
        return ((gradients, square_sum + squares), (result.astype(jnp.bfloat16), grad_stream.astype(jnp.bfloat16)))
    initial = (jax.tree.map(jnp.zeros_like, weights), jnp.zeros((3,), jnp.float32))
    (gradients, square_sum), (layer_out, grad_tokens) = lax.scan(one_slot, initial, (tokens.astype(jnp.float32), cotangent.astype(jnp.float32), keep_all))
    denominator = jnp.sum(slot_lengths).astype(jnp.float32) * D
    stream_rms = jnp.sqrt(square_sum / denominator)
    return (layer_out, grad_tokens, gradients[0], gradients[1], gradients[2], gradients[3], gradients[4], gradients[5], gradients[6], gradients[7], gradients[8], stream_rms)
```

```python
import jax
import jax.numpy as jnp
from jax import lax
from jax.sharding import PartitionSpec as P

HD = 64


epsilon = 1e-12
rope_base = 1000.0
block_limit = 512
direct_limit = 8


def rope_tables(positions, head_size):
    half_size = head_size // 2
    exponent = jnp.arange(half_size, dtype=jnp.float32) * (2.0 / head_size)
    frequency = jnp.power(jnp.float32(rope_base), -exponent)
    angles = positions[:, None] * frequency[None, :]
    cos_half = jnp.cos(angles)
    sin_half = jnp.sin(angles)
    return (
        jnp.concatenate([cos_half, cos_half], axis=-1),
        jnp.concatenate([sin_half, sin_half], axis=-1),
    )


def rotate(values_in, cos_table, sin_table):
    half_size = values_in.shape[-1] // 2
    turned = jnp.concatenate([-values_in[..., half_size:], values_in[..., :half_size]], axis=-1)
    return values_in * cos_table + turned * sin_table


def unrotate(grads_in, cos_table, sin_table):
    scaled = grads_in * sin_table
    half_size = grads_in.shape[-1] // 2
    turned = jnp.concatenate([scaled[..., half_size:], -scaled[..., :half_size]], axis=-1)
    return grads_in * cos_table + turned


def lookup(table, position):
    marks = jnp.arange(table.shape[0], dtype=jnp.int32) == position
    return jnp.sum(jnp.where(marks, table, 0))


def layer_norm(stream, gain_vec, bias_vec):
    average = jnp.mean(stream, axis=-1, keepdims=True)
    centred = stream - average
    variance = jnp.mean(centred * centred, axis=-1, keepdims=True)
    inverse = lax.rsqrt(variance + epsilon)
    normal = centred * inverse
    return (normal * gain_vec + bias_vec, normal, inverse)


def norm_back(grad_rows, normal, inverse, gain_vec):
    scaled = grad_rows * gain_vec
    first_mean = jnp.mean(scaled, axis=-1, keepdims=True)
    second_mean = jnp.mean(scaled * normal, axis=-1, keepdims=True)
    grad_in = (scaled - first_mean - normal * second_mean) * inverse
    return (grad_in, jnp.sum(grad_rows * normal, axis=0), jnp.sum(grad_rows, axis=0))


def flip(array, axis, mask):
    count = lax.axis_size(axis)
    return lax.ppermute(array, axis, [(i, i ^ mask) for i in range(count)])


def spread(block):
    return [block] + [flip(block, "seq", m) for m in range(1, lax.axis_size("seq"))]


def exchange(blocks):
    return [blocks[0]] + [flip(blocks[m], "seq", m) for m in range(1, len(blocks))]


def unmix(blocks, rank):
    stacked = jnp.stack(blocks)
    for m, block in enumerate(blocks):
        stacked = lax.dynamic_update_index_in_dim(stacked, block, rank ^ m, 0)
    return stacked


def gather_rows(shard):
    count = lax.axis_size("fsdp")
    if count > direct_limit:
        return lax.all_gather(shard, "fsdp", axis=0, tiled=True)
    planes = count // 2
    rank = lax.axis_index("fsdp")
    plane = rank // 2
    blocks = [shard] + [
        lax.ppermute(shard, "fsdp", [(i, (i + 2 * k) % count) for i in range(count)])
        for k in range(1, planes)
    ]
    half = jnp.stack(blocks)
    for k, block in enumerate(blocks):
        half = lax.dynamic_update_index_in_dim(half, block, (plane - k) % planes, 0)
    other = flip(half, "fsdp", 1)
    first = (rank % 2) == 0
    pair = jnp.stack([jnp.where(first, half, other), jnp.where(first, other, half)], axis=1)
    return pair.reshape((count * shard.shape[0],) + shard.shape[1:])


def scatter_rows(grad):
    count = lax.axis_size("fsdp")
    if count > direct_limit:
        return lax.psum_scatter(
            grad.astype(jnp.bfloat16), "fsdp", scatter_dimension=0, tiled=True
        ).astype(jnp.float32)
    planes = count // 2
    rank = lax.axis_index("fsdp")
    plane = rank // 2
    rows = grad.shape[0] // count
    view = grad.reshape(planes, 2, rows, grad.shape[1])
    mine = lax.dynamic_index_in_dim(view, rank % 2, 1, keepdims=False)
    theirs = lax.dynamic_index_in_dim(view, 1 - rank % 2, 1, keepdims=False)
    half = mine + flip(theirs.astype(jnp.bfloat16), "fsdp", 1).astype(jnp.float32)
    low = half.astype(jnp.bfloat16)
    total = lax.dynamic_index_in_dim(half, plane, 0, keepdims=False)
    for k in range(1, planes):
        leaving = lax.dynamic_index_in_dim(low, (plane + k) % planes, 0, keepdims=False)
        total = total + lax.ppermute(
            leaving, "fsdp", [(i, (i + 2 * k) % count) for i in range(count)]
        ).astype(jnp.float32)
    return total


def sum_all(array):
    for axis in ("seq", "fsdp"):
        mask = 1
        while mask < lax.axis_size(axis):
            array = array + flip(array, axis, mask)
            mask *= 2
    return array


def total_of(blocks):
    out = blocks[0].astype(jnp.float32)
    for block in blocks[1:]:
        out = out + block.astype(jnp.float32)
    return out


def masked_scores(query_block, key_rows, key_mask, score_scale):
    scores = (
        jnp.einsum("qhe,khe->hqk", query_block, key_rows, preferred_element_type=jnp.float32)
        * score_scale
    )
    return jnp.where(key_mask[None, None, :], scores, -1e30)


def attend(queries, key_rows, values, key_mask, block_count):
    seqlen, head_count, head_size = queries.shape
    block_rows = min(block_limit, seqlen)
    score_scale = head_size ** (-0.5)

    def one_block(block_index, loop_state):
        out_rows, log_totals = loop_state
        offset = block_index * block_rows
        query_block = lax.dynamic_slice_in_dim(queries, offset, block_rows, 0)
        scores = masked_scores(query_block, key_rows, key_mask, score_scale)
        row_max = jnp.max(scores, axis=-1, keepdims=True)
        raised = jnp.exp(scores - row_max)
        row_total = jnp.sum(raised, axis=-1, keepdims=True)
        attn_probs = (raised / row_total).astype(jnp.bfloat16)
        attended = jnp.einsum(
            "hqk,khe->qhe", attn_probs, values, preferred_element_type=jnp.float32
        )
        attended = attended.astype(jnp.bfloat16).reshape(block_rows, head_count * head_size)
        out_rows = lax.dynamic_update_slice_in_dim(out_rows, attended, offset, 0)
        log_totals = lax.dynamic_update_slice_in_dim(
            log_totals, (row_max + jnp.log(row_total))[..., 0], offset, 1
        )
        return (out_rows, log_totals)

    initial = (
        jnp.zeros((seqlen, head_count * head_size), jnp.bfloat16),
        jnp.zeros((head_count, seqlen), jnp.float32),
    )
    return lax.fori_loop(0, block_count, one_block, initial)


def attend_back(queries, key_rows, values, grad_heads, log_totals, key_mask, block_count):
    seqlen, head_count, head_size = queries.shape
    block_rows = min(block_limit, seqlen)
    score_scale = head_size ** (-0.5)
    grad_shaped = grad_heads.reshape(seqlen, head_count, head_size)

    def one_block(block_index, loop_state):
        grad_query, grad_key, grad_value = loop_state
        offset = block_index * block_rows
        query_block = lax.dynamic_slice_in_dim(queries, offset, block_rows, 0)
        grad_block = lax.dynamic_slice_in_dim(grad_shaped, offset, block_rows, 0)
        log_block = lax.dynamic_slice_in_dim(log_totals, offset, block_rows, 1)
        scores = masked_scores(query_block, key_rows, key_mask, score_scale)
        attn_probs = jnp.exp(scores - log_block[..., None])
        grad_probs = jnp.einsum(
            "qhe,khe->hqk", grad_block, values, preferred_element_type=jnp.float32
        )
        row_dot = jnp.sum(attn_probs * grad_probs, axis=-1, keepdims=True)
        grad_scores = (attn_probs * (grad_probs - row_dot)).astype(jnp.bfloat16)
        query_part = (
            jnp.einsum("hqk,khe->qhe", grad_scores, key_rows, preferred_element_type=jnp.float32)
            * score_scale
        )
        grad_query = lax.dynamic_update_slice_in_dim(
            grad_query, query_part.astype(jnp.bfloat16), offset, 0
        )
        grad_key = (
            grad_key
            + jnp.einsum(
                "hqk,qhe->khe", grad_scores, query_block, preferred_element_type=jnp.float32
            )
            * score_scale
        )
        grad_value = grad_value + jnp.einsum(
            "hqk,qhe->khe",
            attn_probs.astype(jnp.bfloat16),
            grad_block,
            preferred_element_type=jnp.float32,
        )
        return (grad_query, grad_key, grad_value)

    initial = (
        jnp.zeros((seqlen, head_count, head_size), jnp.bfloat16),
        jnp.zeros((seqlen, head_count, head_size), jnp.float32),
        jnp.zeros((seqlen, head_count, head_size), jnp.float32),
    )
    grad_query, grad_key, grad_value = lax.fori_loop(0, block_count, one_block, initial)
    return (grad_query, grad_key.astype(jnp.bfloat16), grad_value.astype(jnp.bfloat16))


def body(
    tokens,
    cotangent,
    w_qkv,
    w_out,
    w_gate,
    w_up,
    w_down,
    gain_one,
    bias_one,
    gain_two,
    bias_two,
    seq_lens,
    slot_seq,
):
    parts = lax.axis_size("seq")
    shards = lax.axis_size("fsdp")
    rank = lax.axis_index("seq")
    owner = lax.axis_index("fsdp")
    rows = tokens.shape[1]
    width = tokens.shape[2]
    shard_rows = w_qkv.shape[0]
    heads = width // HD // parts
    head_width = heads * HD
    hidden = w_down.shape[0]
    piece = hidden // parts
    wide = shards * piece
    seqlen = rows * parts
    stream_in = tokens[0]
    length = lookup(seq_lens, lookup(slot_seq, owner))
    own = jnp.arange(rows, dtype=jnp.int32)
    positions = rank * rows + own
    column = (positions < length).astype(jnp.float32)[:, None]
    block_order = jnp.arange(parts, dtype=jnp.int32) ^ rank
    all_positions = (block_order[:, None] * rows + own[None, :]).reshape(seqlen)
    key_mask = all_positions < length
    block_count = seqlen // min(block_limit, seqlen)

    stream_blocks = spread(stream_in)
    qkv_piece = lax.dynamic_index_in_dim(
        w_qkv.reshape(shard_rows, 3, parts, head_width), rank, 2, keepdims=False
    ).reshape(shard_rows, 3 * head_width)
    full_qkv = gather_rows(qkv_piece)

    def columns_of(weight):
        return lax.dynamic_index_in_dim(
            weight.reshape(shard_rows, shards, parts, piece), rank, 2, keepdims=False
        ).reshape(shard_rows, wide)

    vectors = jnp.concatenate([gain_one, bias_one, gain_two, bias_two])
    vectors = jnp.pad(vectors, (0, width - vectors.shape[0])).reshape(1, width)
    out_piece = jnp.concatenate([w_out, jnp.pad(vectors, ((0, 15), (0, 0)))], axis=0)
    down_piece = lax.dynamic_slice_in_dim(w_down, rank * piece, piece, 0)
    ffn_piece = jnp.concatenate(
        [
            columns_of(w_gate),
            columns_of(w_up),
            down_piece,
        ],
        axis=1,
    )
    out_piece, ffn_piece, full_qkv = lax.optimization_barrier((out_piece, ffn_piece, full_qkv))
    gathered_out = gather_rows(out_piece).reshape(shards, shard_rows + 16, width)
    full_out = gathered_out[:, :shard_rows].reshape(width, width)
    params = gathered_out[:, shard_rows, : 4 * shard_rows].astype(jnp.float32)
    params = params.reshape(shards, 4, shard_rows).transpose(1, 0, 2).reshape(4, width)
    gain_first, bias_first, gain_second, bias_second = (params[i : i + 1] for i in range(4))
    full_ffn = gather_rows(ffn_piece)
    full_gate_up = full_ffn[:, : 2 * wide]
    full_down = full_ffn[:, 2 * wide :]

    stream_all = jnp.concatenate(stream_blocks, axis=0)
    projected = jnp.dot(stream_all, full_qkv, preferred_element_type=jnp.float32).reshape(
        seqlen, 3, heads, HD
    )
    cos_table, sin_table = rope_tables(all_positions.astype(jnp.float32), HD)
    cos_table = cos_table[:, None, :]
    sin_table = sin_table[:, None, :]
    queries = rotate(projected[:, 0], cos_table, sin_table).astype(jnp.bfloat16)
    key_rows = rotate(projected[:, 1], cos_table, sin_table).astype(jnp.bfloat16)
    values = projected[:, 2].astype(jnp.bfloat16)
    head_out, log_totals = attend(queries, key_rows, values, key_mask, block_count)
    mixed = exchange([head_out[m * rows : (m + 1) * rows] for m in range(parts)])
    head_mix = unmix(mixed, rank).transpose(1, 0, 2).reshape(rows, width)
    branch_attn = jnp.dot(head_mix, full_out, preferred_element_type=jnp.float32)
    stream_float = stream_in.astype(jnp.float32)
    normed_float, normal_one, inverse_one = layer_norm(
        stream_float + branch_attn, gain_first, bias_first
    )
    normed_one = normed_float.astype(jnp.bfloat16)
    normed_all = jnp.concatenate(spread(normed_one), axis=0)
    gate_up = jnp.dot(normed_all, full_gate_up, preferred_element_type=jnp.float32)
    gate_proj = gate_up[:, :wide]
    up_proj = gate_up[:, wide:]
    inner_act = (jax.nn.silu(gate_proj) * up_proj).astype(jnp.bfloat16)
    ffn_part = jnp.dot(inner_act, full_down, preferred_element_type=jnp.float32).astype(
        jnp.bfloat16
    )
    branch_ffn = total_of(exchange([ffn_part[m * rows : (m + 1) * rows] for m in range(parts)]))
    out_float, normal_two, inverse_two = layer_norm(
        normed_one.astype(jnp.float32) + branch_ffn, gain_second, bias_second
    )
    layer_out = (out_float * column).astype(jnp.bfloat16)
    grad_rows = cotangent[0].astype(jnp.float32) * column
    grad_two, gain_two_grad, bias_two_grad = norm_back(
        grad_rows, normal_two, inverse_two, gain_second
    )
    grad_ffn = grad_two.astype(jnp.bfloat16)
    grad_ffn_all = jnp.concatenate(spread(grad_ffn), axis=0)
    grad_inner = jnp.einsum("td,fd->tf", grad_ffn_all, full_down, preferred_element_type=jnp.float32)
    sigmoid_gate = jax.nn.sigmoid(gate_proj)
    grad_gate_rows = (
        grad_inner * up_proj * sigmoid_gate * (1.0 + gate_proj * (1.0 - sigmoid_gate))
    ).astype(jnp.bfloat16)
    grad_up_rows = (grad_inner * gate_proj * sigmoid_gate).astype(jnp.bfloat16)
    grad_both = jnp.concatenate([grad_gate_rows, grad_up_rows], axis=1)
    normed_part = jnp.einsum(
        "tf,df->td", grad_both, full_gate_up, preferred_element_type=jnp.float32
    ).astype(jnp.bfloat16)
    grad_normed = (
        total_of(exchange([normed_part[m * rows : (m + 1) * rows] for m in range(parts)])) + grad_two
    )
    down_grad = jnp.einsum("tf,td->fd", inner_act, grad_ffn_all, preferred_element_type=jnp.float32)
    both_grad = jnp.einsum("td,tf->df", normed_all, grad_both, preferred_element_type=jnp.float32)
    ffn_grad = scatter_rows(jnp.concatenate([both_grad, down_grad], axis=1))

    grad_one, gain_one_grad, bias_one_grad = norm_back(
        grad_normed, normal_one, inverse_one, gain_first
    )
    squares = jnp.concatenate(
        [
            jnp.sum(column * stream_float * stream_float, axis=0, keepdims=True),
            jnp.sum(column * branch_attn * branch_attn, axis=0, keepdims=True),
            jnp.sum(column * branch_ffn * branch_ffn, axis=0, keepdims=True),
            gain_one_grad[None],
            bias_one_grad[None],
            gain_two_grad[None],
            bias_two_grad[None],
            jnp.zeros((1, width), jnp.float32),
        ],
        axis=0,
    )
    sums = sum_all(squares)
    denominator = jnp.sum(seq_lens).astype(jnp.float32) * width
    stream_rms = jnp.sqrt(jnp.sum(sums[:3], axis=1) / denominator)
    vector_grads = lax.dynamic_index_in_dim(
        sums[3:7].reshape(4, shards, shard_rows), owner, 1, keepdims=False
    )

    grad_attn = grad_one.astype(jnp.bfloat16)
    grad_mix = (
        jnp.einsum("te,de->td", grad_attn, full_out, preferred_element_type=jnp.float32)
        .astype(jnp.bfloat16)
        .reshape(rows, parts, head_width)
        .transpose(1, 0, 2)
    )
    leaving = [
        lax.dynamic_index_in_dim(grad_mix, rank ^ m, 0, keepdims=False) for m in range(parts)
    ]
    grad_heads = jnp.concatenate(exchange(leaving), axis=0)
    out_grad = scatter_rows(
        jnp.einsum("td,te->de", head_mix, grad_attn, preferred_element_type=jnp.float32)
    )
    grad_query, grad_key, grad_value = attend_back(
        queries, key_rows, values, grad_heads, log_totals, key_mask, block_count
    )
    grad_proj = jnp.stack(
        [
            unrotate(grad_query.astype(jnp.float32), cos_table, sin_table),
            unrotate(grad_key.astype(jnp.float32), cos_table, sin_table),
            grad_value.astype(jnp.float32),
        ],
        axis=1,
    )
    grad_proj = grad_proj.astype(jnp.bfloat16).reshape(seqlen, 3 * head_width)
    token_part = jnp.einsum(
        "tc,dc->td", grad_proj, full_qkv, preferred_element_type=jnp.float32
    ).astype(jnp.bfloat16)
    grad_tokens = (
        total_of(exchange([token_part[m * rows : (m + 1) * rows] for m in range(parts)])) + grad_one
    ).astype(jnp.bfloat16)
    qkv_grad = scatter_rows(
        jnp.einsum("td,tc->dc", stream_all, grad_proj, preferred_element_type=jnp.float32)
    )
    qkv_blocks = unmix(spread(qkv_grad.astype(jnp.bfloat16)), rank).astype(jnp.float32)
    qkv_out = (
        qkv_blocks.reshape(parts, shard_rows, 3, head_width)
        .transpose(1, 2, 0, 3)
        .reshape(shard_rows, 3 * width)
    )
    ffn_blocks = unmix(spread(ffn_grad.astype(jnp.bfloat16)), rank).astype(jnp.float32)

    def restore(blocks):
        return (
            blocks.reshape(parts, shard_rows, shards, piece)
            .transpose(1, 2, 0, 3)
            .reshape(shard_rows, shards * hidden)
        )

    gate_out = restore(ffn_blocks[:, :, :wide])
    up_out = restore(ffn_blocks[:, :, wide : 2 * wide])
    down_out = ffn_blocks[:, :, 2 * wide :].reshape(hidden, width)
    out_split = out_grad.astype(jnp.bfloat16).reshape(parts, shard_rows // parts, width)
    out_sum = total_of(
        exchange(
            [lax.dynamic_index_in_dim(out_split, rank ^ m, 0, keepdims=False) for m in range(parts)]
        )
    )
    out_out = (
        unmix(spread(out_sum.astype(jnp.bfloat16)), rank)
        .astype(jnp.float32)
        .reshape(shard_rows, width)
    )
    return (
        layer_out[None],
        grad_tokens[None],
        qkv_out,
        out_out,
        gate_out,
        up_out,
        down_out,
        vector_grads[0],
        vector_grads[1],
        vector_grads[2],
        vector_grads[3],
        stream_rms,
    )


def solution(mesh):
    placed = (
        P("fsdp", "seq", None),
        P("fsdp", "seq", None),
        P("fsdp", None),
        P("fsdp", None),
        P("fsdp", None),
        P("fsdp", None),
        P("fsdp", None),
        P("fsdp"),
        P("fsdp"),
        P("fsdp"),
        P("fsdp"),
        P(),
        P(),
    )
    return jax.shard_map(
        body,
        mesh=mesh,
        in_specs=placed,
        out_specs=(
            P("fsdp", "seq", None),
            P("fsdp", "seq", None),
            P("fsdp", None),
            P("fsdp", None),
            P("fsdp", None),
            P("fsdp", None),
            P("fsdp", None),
            P("fsdp"),
            P("fsdp"),
            P("fsdp"),
            P("fsdp"),
            P(),
        ),
        check_vma=False,
    )
```

```python
import functools

import jax
import jax.numpy as jnp
from jax import lax
from jax.experimental import pallas as pl
from jax.experimental.pallas import tpu as pltpu
from jax.sharding import PartitionSpec as P

HD = 64


epsilon = 1e-12
rope_base = 1000.0
direct_limit = 8


def rope_tables(positions, head_size):
    half_size = head_size // 2
    exponent = jnp.arange(half_size, dtype=jnp.float32) * (2.0 / head_size)
    frequency = jnp.power(jnp.float32(rope_base), -exponent)
    angles = positions[:, None] * frequency[None, :]
    cos_half = jnp.cos(angles)
    sin_half = jnp.sin(angles)
    return (
        jnp.concatenate([cos_half, cos_half], axis=-1),
        jnp.concatenate([sin_half, sin_half], axis=-1),
    )


def rotate(values_in, cos_table, sin_table):
    half_size = values_in.shape[-1] // 2
    turned = jnp.concatenate([-values_in[..., half_size:], values_in[..., :half_size]], axis=-1)
    return values_in * cos_table + turned * sin_table


def unrotate(grads_in, cos_table, sin_table):
    scaled = grads_in * sin_table
    half_size = grads_in.shape[-1] // 2
    turned = jnp.concatenate([scaled[..., half_size:], -scaled[..., :half_size]], axis=-1)
    return grads_in * cos_table + turned


def lookup(table, position):
    marks = jnp.arange(table.shape[0], dtype=jnp.int32) == position
    return jnp.sum(jnp.where(marks, table, 0))


def layer_norm(stream, gain_vec, bias_vec):
    average = jnp.mean(stream, axis=-1, keepdims=True)
    centred = stream - average
    variance = jnp.mean(centred * centred, axis=-1, keepdims=True)
    inverse = lax.rsqrt(variance + epsilon)
    normal = centred * inverse
    return (normal * gain_vec + bias_vec, normal, inverse)


def norm_back(grad_rows, normal, inverse, gain_vec):
    scaled = grad_rows * gain_vec
    first_mean = jnp.mean(scaled, axis=-1, keepdims=True)
    second_mean = jnp.mean(scaled * normal, axis=-1, keepdims=True)
    grad_in = (scaled - first_mean - normal * second_mean) * inverse
    return (grad_in, jnp.sum(grad_rows * normal, axis=0), jnp.sum(grad_rows, axis=0))


def flip(array, axis, mask):
    count = lax.axis_size(axis)
    return lax.ppermute(array, axis, [(i, i ^ mask) for i in range(count)])


def spread(block):
    return [block] + [flip(block, "seq", m) for m in range(1, lax.axis_size("seq"))]


def exchange(blocks):
    return [blocks[0]] + [flip(blocks[m], "seq", m) for m in range(1, len(blocks))]


def unmix(blocks, rank):
    stacked = jnp.stack(blocks)
    for m, block in enumerate(blocks):
        stacked = lax.dynamic_update_index_in_dim(stacked, block, rank ^ m, 0)
    return stacked


def gather_rows(shard):
    count = lax.axis_size("fsdp")
    if count > direct_limit:
        return lax.all_gather(shard, "fsdp", axis=0, tiled=True)
    planes = count // 2
    rank = lax.axis_index("fsdp")
    plane = rank // 2
    blocks = [shard] + [
        lax.ppermute(shard, "fsdp", [(i, (i + 2 * k) % count) for i in range(count)])
        for k in range(1, planes)
    ]
    half = jnp.stack(blocks)
    for k, block in enumerate(blocks):
        half = lax.dynamic_update_index_in_dim(half, block, (plane - k) % planes, 0)
    other = flip(half, "fsdp", 1)
    first = (rank % 2) == 0
    pair = jnp.stack([jnp.where(first, half, other), jnp.where(first, other, half)], axis=1)
    return pair.reshape((count * shard.shape[0],) + shard.shape[1:])


def scatter_rows(grad):
    count = lax.axis_size("fsdp")
    if count > direct_limit:
        return lax.psum_scatter(
            grad.astype(jnp.bfloat16), "fsdp", scatter_dimension=0, tiled=True
        ).astype(jnp.float32)
    planes = count // 2
    rank = lax.axis_index("fsdp")
    plane = rank // 2
    rows = grad.shape[0] // count
    view = grad.reshape(planes, 2, rows, grad.shape[1])
    mine = lax.dynamic_index_in_dim(view, rank % 2, 1, keepdims=False)
    theirs = lax.dynamic_index_in_dim(view, 1 - rank % 2, 1, keepdims=False)
    half = mine + flip(theirs.astype(jnp.bfloat16), "fsdp", 1).astype(jnp.float32)
    low = half.astype(jnp.bfloat16)
    total = lax.dynamic_index_in_dim(half, plane, 0, keepdims=False)
    for k in range(1, planes):
        leaving = lax.dynamic_index_in_dim(low, (plane + k) % planes, 0, keepdims=False)
        total = total + lax.ppermute(
            leaving, "fsdp", [(i, (i + 2 * k) % count) for i in range(count)]
        ).astype(jnp.float32)
    return total


def sum_all(array):
    for axis in ("seq", "fsdp"):
        mask = 1
        while mask < lax.axis_size(axis):
            array = array + flip(array, axis, mask)
            mask *= 2
    return array


def total_of(blocks):
    out = blocks[0].astype(jnp.float32)
    for block in blocks[1:]:
        out = out + block.astype(jnp.float32)
    return out


tile = 256
log2e = 1.4426950408889634


def turn(left, right):
    return lax.dot_general(left, right, (((1,), (1,)), ((), ())), preferred_element_type=jnp.float32)


def times(left, right):
    return lax.dot_general(left, right, (((1,), (0,)), ((), ())), preferred_element_type=jnp.float32)


def valid_keys(info, key_tile, size):
    base = (info[0] ^ key_tile) * size
    return lax.broadcasted_iota(jnp.int32, (size, size), 0) < (info[1] - base)


def attend_kernel(heads, info, qkv, out, log_rows, scores):
    seqlen = qkv.shape[0]
    blocks = seqlen // tile
    width = heads * HD
    for h in range(heads):
        value_cols = qkv[:, 2 * width + h * HD : 2 * width + (h + 1) * HD]
        value_turned = value_cols.T

        def one_block(i, carry, h=h, value_turned=value_turned):
            rows = pl.ds(pl.multiple_of(i * tile, tile), tile)
            query = qkv[rows, h * HD : (h + 1) * HD]
            tops = None
            for j in range(blocks):
                keys = qkv[j * tile : (j + 1) * tile, width + h * HD : width + (h + 1) * HD]
                part = jnp.where(valid_keys(info, j, tile), turn(keys, query), -1e30)
                scores[j * tile : (j + 1) * tile, :] = part
                top = jnp.max(part, axis=0, keepdims=True)
                tops = top if tops is None else jnp.maximum(tops, top)
            mixed = None
            total = None
            for j in range(blocks):
                raised = jnp.exp2(
                    (scores[j * tile : (j + 1) * tile, :] - tops) * (log2e * HD ** (-0.5))
                )
                part = jnp.sum(raised, axis=0, keepdims=True)
                total = part if total is None else total + part
                piece = times(
                    value_turned[:, j * tile : (j + 1) * tile], raised.astype(jnp.bfloat16)
                )
                mixed = piece if mixed is None else mixed + piece
            out[rows, h * HD : (h + 1) * HD] = (mixed / total).T.astype(jnp.bfloat16)
            log_rows[h : h + 1, rows] = tops * (log2e * HD ** (-0.5)) + jnp.log2(total)
            return carry

        lax.fori_loop(0, blocks, one_block, 0)


def attend_back_kernel(heads, info, qkv, mixed, grads, log_rows, out, key_sum, value_sum):
    seqlen = qkv.shape[0]
    blocks = seqlen // tile
    width = heads * HD
    scale = HD ** (-0.5)
    for h in range(heads):
        low, high = h * HD, (h + 1) * HD
        key_turned = qkv[:, width + low : width + high].T
        key_sum[...] = jnp.zeros_like(key_sum)
        value_sum[...] = jnp.zeros_like(value_sum)

        def one_block(i, carry, low=low, high=high, h=h, key_turned=key_turned):
            rows = pl.ds(pl.multiple_of(i * tile, tile), tile)
            query = qkv[rows, low:high]
            grad = grads[rows, low:high]
            row_dot = jnp.sum(
                (grad.astype(jnp.float32) * mixed[rows, low:high].astype(jnp.float32)).T,
                axis=0,
                keepdims=True,
            )
            logs = log_rows[h : h + 1, rows]
            query_grad = None
            for j in range(blocks):
                span = slice(j * tile, (j + 1) * tile)
                keys = qkv[span, width + low : width + high]
                values = qkv[span, 2 * width + low : 2 * width + high]
                probs = jnp.where(
                    valid_keys(info, j, tile),
                    jnp.exp2(turn(keys, query) * (log2e * HD ** (-0.5)) - logs),
                    0.0,
                )
                grad_scores = (probs * (turn(values, grad) - row_dot)).astype(jnp.bfloat16)
                value_sum[span, :] += times(probs.astype(jnp.bfloat16), grad)
                key_sum[span, :] += times(grad_scores, query)
                piece = times(key_turned[:, span], grad_scores)
                query_grad = piece if query_grad is None else query_grad + piece
            out[rows, low:high] = (query_grad * scale).T.astype(jnp.bfloat16)
            return carry

        lax.fori_loop(0, blocks, one_block, 0)
        out[:, width + low : width + high] = (key_sum[...] * scale).astype(jnp.bfloat16)
        out[:, 2 * width + low : 2 * width + high] = value_sum[...].astype(jnp.bfloat16)


def attend(info, qkv, heads):
    seqlen = qkv.shape[0]
    whole = pl.BlockSpec(memory_space=pltpu.VMEM)
    return pl.pallas_call(
        functools.partial(attend_kernel, heads),
        out_shape=(
            jax.ShapeDtypeStruct((seqlen, heads * HD), jnp.bfloat16),
            jax.ShapeDtypeStruct((8, seqlen), jnp.float32),
        ),
        in_specs=[pl.BlockSpec(memory_space=pltpu.SMEM), whole],
        out_specs=(whole, whole),
        scratch_shapes=[pltpu.VMEM((seqlen, tile), jnp.float32)],
        cost_estimate=pl.CostEstimate(
            flops=16 * heads * seqlen * seqlen * HD, bytes_accessed=8 * seqlen * heads * HD,
            transcendentals=heads * seqlen * seqlen,
        ),
        name="attend",
    )(info, qkv)


def attend_back(info, qkv, mixed, grads, log_rows, heads):
    seqlen = qkv.shape[0]
    whole = pl.BlockSpec(memory_space=pltpu.VMEM)
    return pl.pallas_call(
        functools.partial(attend_back_kernel, heads),
        out_shape=jax.ShapeDtypeStruct((seqlen, 3 * heads * HD), jnp.bfloat16),
        in_specs=[pl.BlockSpec(memory_space=pltpu.SMEM), whole, whole, whole, whole],
        out_specs=whole,
        scratch_shapes=[
            pltpu.VMEM((seqlen, HD), jnp.float32),
            pltpu.VMEM((seqlen, HD), jnp.float32),
        ],
        cost_estimate=pl.CostEstimate(
            flops=40 * heads * seqlen * seqlen * HD, bytes_accessed=16 * seqlen * heads * HD,
            transcendentals=heads * seqlen * seqlen,
        ),
        name="attend_back",
    )(info, qkv, mixed, grads, log_rows)


def body(
    tokens,
    cotangent,
    w_qkv,
    w_out,
    w_gate,
    w_up,
    w_down,
    gain_one,
    bias_one,
    gain_two,
    bias_two,
    seq_lens,
    slot_seq,
):
    parts = lax.axis_size("seq")
    shards = lax.axis_size("fsdp")
    rank = lax.axis_index("seq")
    owner = lax.axis_index("fsdp")
    rows = tokens.shape[1]
    width = tokens.shape[2]
    shard_rows = w_qkv.shape[0]
    heads = width // HD // parts
    head_width = heads * HD
    hidden = w_down.shape[0]
    piece = hidden // parts
    wide = shards * piece
    seqlen = rows * parts
    stream_in = tokens[0]
    length = lookup(seq_lens, lookup(slot_seq, owner))
    own = jnp.arange(rows, dtype=jnp.int32)
    positions = rank * rows + own
    column = (positions < length).astype(jnp.float32)[:, None]
    block_order = jnp.arange(parts, dtype=jnp.int32) ^ rank
    all_positions = (block_order[:, None] * rows + own[None, :]).reshape(seqlen)
    info = jnp.stack([rank.astype(jnp.int32), length.astype(jnp.int32)])

    stream_blocks = spread(stream_in)
    qkv_piece = lax.dynamic_index_in_dim(
        w_qkv.reshape(shard_rows, 3, parts, head_width), rank, 2, keepdims=False
    ).reshape(shard_rows, 3 * head_width)
    full_qkv = gather_rows(qkv_piece)

    def columns_of(weight):
        return lax.dynamic_index_in_dim(
            weight.reshape(shard_rows, shards, parts, piece), rank, 2, keepdims=False
        ).reshape(shard_rows, wide)

    vectors = jnp.concatenate([gain_one, bias_one, gain_two, bias_two])
    vectors = jnp.pad(vectors, (0, width - vectors.shape[0])).reshape(1, width)
    out_piece = jnp.concatenate([w_out, jnp.pad(vectors, ((0, 15), (0, 0)))], axis=0)
    down_piece = lax.dynamic_slice_in_dim(w_down, rank * piece, piece, 0)
    ffn_piece = jnp.concatenate(
        [
            columns_of(w_gate),
            columns_of(w_up),
            down_piece,
        ],
        axis=1,
    )
    out_piece, ffn_piece, full_qkv = lax.optimization_barrier((out_piece, ffn_piece, full_qkv))
    gathered_out = gather_rows(out_piece).reshape(shards, shard_rows + 16, width)
    full_out = gathered_out[:, :shard_rows].reshape(width, width)
    params = gathered_out[:, shard_rows, : 4 * shard_rows].astype(jnp.float32)
    params = params.reshape(shards, 4, shard_rows).transpose(1, 0, 2).reshape(4, width)
    gain_first, bias_first, gain_second, bias_second = (params[i : i + 1] for i in range(4))
    full_ffn = gather_rows(ffn_piece)
    full_gate_up = full_ffn[:, : 2 * wide]
    full_down = full_ffn[:, 2 * wide :]

    stream_all = jnp.concatenate(stream_blocks, axis=0)
    projected = jnp.dot(stream_all, full_qkv, preferred_element_type=jnp.float32).reshape(
        seqlen, 3, heads, HD
    )
    cos_table, sin_table = rope_tables(all_positions.astype(jnp.float32), HD)
    cos_table = cos_table[:, None, :]
    sin_table = sin_table[:, None, :]
    queries = rotate(projected[:, 0], cos_table, sin_table).astype(jnp.bfloat16)
    key_rows = rotate(projected[:, 1], cos_table, sin_table).astype(jnp.bfloat16)
    values = projected[:, 2].astype(jnp.bfloat16)
    qkv_rows = jnp.stack([queries, key_rows, values], axis=1).reshape(seqlen, 3 * head_width)
    head_out, log_rows = attend(info, qkv_rows, heads)
    mixed = exchange([head_out[m * rows : (m + 1) * rows] for m in range(parts)])
    head_mix = unmix(mixed, rank).transpose(1, 0, 2).reshape(rows, width)
    branch_attn = jnp.dot(head_mix, full_out, preferred_element_type=jnp.float32)
    stream_float = stream_in.astype(jnp.float32)
    normed_float, normal_one, inverse_one = layer_norm(
        stream_float + branch_attn, gain_first, bias_first
    )
    normed_one = normed_float.astype(jnp.bfloat16)
    normed_all = jnp.concatenate(spread(normed_one), axis=0)
    gate_up = jnp.dot(normed_all, full_gate_up, preferred_element_type=jnp.float32)
    gate_proj = gate_up[:, :wide]
    up_proj = gate_up[:, wide:]
    inner_act = (jax.nn.silu(gate_proj) * up_proj).astype(jnp.bfloat16)
    ffn_part = jnp.dot(inner_act, full_down, preferred_element_type=jnp.float32).astype(
        jnp.bfloat16
    )
    branch_ffn = total_of(exchange([ffn_part[m * rows : (m + 1) * rows] for m in range(parts)]))
    out_float, normal_two, inverse_two = layer_norm(
        normed_one.astype(jnp.float32) + branch_ffn, gain_second, bias_second
    )
    layer_out = (out_float * column).astype(jnp.bfloat16)
    grad_rows = cotangent[0].astype(jnp.float32) * column
    grad_two, gain_two_grad, bias_two_grad = norm_back(
        grad_rows, normal_two, inverse_two, gain_second
    )
    grad_ffn = grad_two.astype(jnp.bfloat16)
    grad_ffn_all = jnp.concatenate(spread(grad_ffn), axis=0)
    grad_inner = jnp.einsum("td,fd->tf", grad_ffn_all, full_down, preferred_element_type=jnp.float32)
    sigmoid_gate = jax.nn.sigmoid(gate_proj)
    grad_gate_rows = (
        grad_inner * up_proj * sigmoid_gate * (1.0 + gate_proj * (1.0 - sigmoid_gate))
    ).astype(jnp.bfloat16)
    grad_up_rows = (grad_inner * gate_proj * sigmoid_gate).astype(jnp.bfloat16)
    grad_both = jnp.concatenate([grad_gate_rows, grad_up_rows], axis=1)
    normed_part = jnp.einsum(
        "tf,df->td", grad_both, full_gate_up, preferred_element_type=jnp.float32
    ).astype(jnp.bfloat16)
    grad_normed = (
        total_of(exchange([normed_part[m * rows : (m + 1) * rows] for m in range(parts)])) + grad_two
    )
    down_grad = jnp.einsum("tf,td->fd", inner_act, grad_ffn_all, preferred_element_type=jnp.float32)
    both_grad = jnp.einsum("td,tf->df", normed_all, grad_both, preferred_element_type=jnp.float32)
    ffn_grad = scatter_rows(jnp.concatenate([both_grad, down_grad], axis=1))

    grad_one, gain_one_grad, bias_one_grad = norm_back(
        grad_normed, normal_one, inverse_one, gain_first
    )
    squares = jnp.concatenate(
        [
            jnp.sum(column * stream_float * stream_float, axis=0, keepdims=True),
            jnp.sum(column * branch_attn * branch_attn, axis=0, keepdims=True),
            jnp.sum(column * branch_ffn * branch_ffn, axis=0, keepdims=True),
            gain_one_grad[None],
            bias_one_grad[None],
            gain_two_grad[None],
            bias_two_grad[None],
            jnp.zeros((1, width), jnp.float32),
        ],
        axis=0,
    )
    sums = sum_all(squares)
    denominator = jnp.sum(seq_lens).astype(jnp.float32) * width
    stream_rms = jnp.sqrt(jnp.sum(sums[:3], axis=1) / denominator)
    vector_grads = lax.dynamic_index_in_dim(
        sums[3:7].reshape(4, shards, shard_rows), owner, 1, keepdims=False
    )

    grad_attn = grad_one.astype(jnp.bfloat16)
    grad_mix = (
        jnp.einsum("te,de->td", grad_attn, full_out, preferred_element_type=jnp.float32)
        .astype(jnp.bfloat16)
        .reshape(rows, parts, head_width)
        .transpose(1, 0, 2)
    )
    leaving = [
        lax.dynamic_index_in_dim(grad_mix, rank ^ m, 0, keepdims=False) for m in range(parts)
    ]
    grad_heads = jnp.concatenate(exchange(leaving), axis=0)
    out_grad = scatter_rows(
        jnp.einsum("td,te->de", head_mix, grad_attn, preferred_element_type=jnp.float32)
    )
    grad_qkv = attend_back(info, qkv_rows, head_out, grad_heads, log_rows, heads).reshape(
        seqlen, 3, heads, HD
    )
    grad_proj = jnp.stack(
        [
            unrotate(grad_qkv[:, 0].astype(jnp.float32), cos_table, sin_table),
            unrotate(grad_qkv[:, 1].astype(jnp.float32), cos_table, sin_table),
            grad_qkv[:, 2].astype(jnp.float32),
        ],
        axis=1,
    )
    grad_proj = grad_proj.astype(jnp.bfloat16).reshape(seqlen, 3 * head_width)
    token_part = jnp.einsum(
        "tc,dc->td", grad_proj, full_qkv, preferred_element_type=jnp.float32
    ).astype(jnp.bfloat16)
    grad_tokens = (
        total_of(exchange([token_part[m * rows : (m + 1) * rows] for m in range(parts)])) + grad_one
    ).astype(jnp.bfloat16)
    qkv_grad = scatter_rows(
        jnp.einsum("td,tc->dc", stream_all, grad_proj, preferred_element_type=jnp.float32)
    )
    qkv_blocks = unmix(spread(qkv_grad.astype(jnp.bfloat16)), rank).astype(jnp.float32)
    qkv_out = (
        qkv_blocks.reshape(parts, shard_rows, 3, head_width)
        .transpose(1, 2, 0, 3)
        .reshape(shard_rows, 3 * width)
    )
    ffn_blocks = unmix(spread(ffn_grad.astype(jnp.bfloat16)), rank).astype(jnp.float32)

    def restore(blocks):
        return (
            blocks.reshape(parts, shard_rows, shards, piece)
            .transpose(1, 2, 0, 3)
            .reshape(shard_rows, shards * hidden)
        )

    gate_out = restore(ffn_blocks[:, :, :wide])
    up_out = restore(ffn_blocks[:, :, wide : 2 * wide])
    down_out = ffn_blocks[:, :, 2 * wide :].reshape(hidden, width)
    out_split = out_grad.astype(jnp.bfloat16).reshape(parts, shard_rows // parts, width)
    out_sum = total_of(
        exchange(
            [lax.dynamic_index_in_dim(out_split, rank ^ m, 0, keepdims=False) for m in range(parts)]
        )
    )
    out_out = (
        unmix(spread(out_sum.astype(jnp.bfloat16)), rank)
        .astype(jnp.float32)
        .reshape(shard_rows, width)
    )
    return (
        layer_out[None],
        grad_tokens[None],
        qkv_out,
        out_out,
        gate_out,
        up_out,
        down_out,
        vector_grads[0],
        vector_grads[1],
        vector_grads[2],
        vector_grads[3],
        stream_rms,
    )


def solution(mesh):
    placed = (
        P("fsdp", "seq", None),
        P("fsdp", "seq", None),
        P("fsdp", None),
        P("fsdp", None),
        P("fsdp", None),
        P("fsdp", None),
        P("fsdp", None),
        P("fsdp"),
        P("fsdp"),
        P("fsdp"),
        P("fsdp"),
        P(),
        P(),
    )
    return jax.shard_map(
        body,
        mesh=mesh,
        in_specs=placed,
        out_specs=(
            P("fsdp", "seq", None),
            P("fsdp", "seq", None),
            P("fsdp", None),
            P("fsdp", None),
            P("fsdp", None),
            P("fsdp", None),
            P("fsdp", None),
            P("fsdp"),
            P("fsdp"),
            P("fsdp"),
            P("fsdp"),
            P(),
        ),
        check_vma=False,
    )
```

```python
import functools

import jax
import jax.numpy as jnp
from jax import lax
from jax.experimental import pallas as pl
from jax.experimental.pallas import tpu as pltpu
from jax.sharding import PartitionSpec as P


HD = 64


epsilon = 1e-12
rope_base = 1000.0
direct_limit = 8


def rope_tables(positions, head_size):
    half_size = head_size // 2
    exponent = jnp.arange(half_size, dtype=jnp.float32) * (2.0 / head_size)
    frequency = jnp.power(jnp.float32(rope_base), -exponent)
    angles = positions[:, None] * frequency[None, :]
    cos_half = jnp.cos(angles)
    sin_half = jnp.sin(angles)
    return (
        jnp.concatenate([cos_half, cos_half], axis=-1),
        jnp.concatenate([sin_half, sin_half], axis=-1),
    )


def rotate(values_in, cos_table, sin_table):
    half_size = values_in.shape[-1] // 2
    turned = jnp.concatenate([-values_in[..., half_size:], values_in[..., :half_size]], axis=-1)
    return values_in * cos_table + turned * sin_table


def unrotate(grads_in, cos_table, sin_table):
    scaled = grads_in * sin_table
    half_size = grads_in.shape[-1] // 2
    turned = jnp.concatenate([scaled[..., half_size:], -scaled[..., :half_size]], axis=-1)
    return grads_in * cos_table + turned


def lookup(table, position):
    marks = jnp.arange(table.shape[0], dtype=jnp.int32) == position
    return jnp.sum(jnp.where(marks, table, 0))


def layer_norm(stream, gain_vec, bias_vec):
    average = jnp.mean(stream, axis=-1, keepdims=True)
    centred = stream - average
    variance = jnp.mean(centred * centred, axis=-1, keepdims=True)
    inverse = lax.rsqrt(variance + epsilon)
    normal = centred * inverse
    return (normal * gain_vec + bias_vec, normal, inverse)


def norm_back(grad_rows, normal, inverse, gain_vec):
    scaled = grad_rows * gain_vec
    first_mean = jnp.mean(scaled, axis=-1, keepdims=True)
    second_mean = jnp.mean(scaled * normal, axis=-1, keepdims=True)
    grad_in = (scaled - first_mean - normal * second_mean) * inverse
    return (grad_in, jnp.sum(grad_rows * normal, axis=0), jnp.sum(grad_rows, axis=0))


def flip(array, axis, mask):
    count = lax.axis_size(axis)
    return lax.ppermute(array, axis, [(i, i ^ mask) for i in range(count)])


def spread(block):
    return [block] + [flip(block, "seq", m) for m in range(1, lax.axis_size("seq"))]


def exchange(blocks):
    return [blocks[0]] + [flip(blocks[m], "seq", m) for m in range(1, len(blocks))]


def unmix(blocks, rank):
    stacked = jnp.stack(blocks)
    for m, block in enumerate(blocks):
        stacked = lax.dynamic_update_index_in_dim(stacked, block, rank ^ m, 0)
    return stacked


def place_kernel(count, order, *refs):
    out, sems = refs[count], refs[count + 1]
    copies = [
        pltpu.make_async_copy(refs[k], out.at[order[k]], sems.at[k]) for k in range(count)
    ]
    for copy in copies:
        copy.start()
    for copy in copies:
        copy.wait()


def place(blocks, order):
    count = len(blocks)
    shape = blocks[0].shape
    return pl.pallas_call(
        functools.partial(place_kernel, count),
        out_shape=jax.ShapeDtypeStruct((count,) + shape, blocks[0].dtype),
        in_specs=[pl.BlockSpec(memory_space=pltpu.SMEM)]
        + [pl.BlockSpec(memory_space=pl.ANY)] * count,
        out_specs=pl.BlockSpec(memory_space=pltpu.VMEM),
        scratch_shapes=[pltpu.SemaphoreType.DMA((count,))],
        name="place",
    )(order, *blocks)


def gather_rows(shard):
    count = lax.axis_size("fsdp")
    if count > direct_limit:
        return lax.all_gather(shard, "fsdp", axis=0, tiled=False), []
    planes = count // 2
    owner = lax.axis_index("fsdp")
    plane = owner >> 1
    core = owner & 1
    blocks = [shard] + [
        lax.ppermute(shard, "fsdp", [(i, (i + 2 * k) % count) for i in range(count)])
        for k in range(1, planes)
    ]
    swapped = [flip(block, "fsdp", 1) for block in blocks]
    origin = 2 * ((plane - jnp.arange(planes, dtype=jnp.int32)) & (planes - 1))
    order = jnp.concatenate([origin + core, origin + 1 - core])
    return place(blocks + swapped, order), blocks[1:]


def scatter_rows(grad):
    count = lax.axis_size("fsdp")
    if count > direct_limit:
        return lax.psum_scatter(grad, "fsdp", scatter_dimension=0, tiled=True).astype(jnp.float32)
    planes = count // 2
    owner = lax.axis_index("fsdp")
    plane = owner >> 1
    core = owner & 1
    view = grad.reshape(count, grad.shape[0] // count, grad.shape[1])

    def part(k, side):
        place_at = 2 * ((plane + k) & (planes - 1)) + (core ^ side)
        return lax.dynamic_index_in_dim(view, place_at, 0, keepdims=False)

    halves = {}
    for k in list(range(1, planes)) + [0]:
        halves[k] = part(k, 0).astype(jnp.float32) + flip(part(k, 1), "fsdp", 1).astype(jnp.float32)
    total = halves[0]
    for k in range(1, planes):
        total = total + lax.ppermute(
            halves[k].astype(jnp.bfloat16), "fsdp", [(i, (i + 2 * k) % count) for i in range(count)]
        ).astype(jnp.float32)
    return total


def restore_kernel(parts, groups, piece, info, *refs):
    blocks, (gate, up, down), (held, sems) = refs[:parts], refs[parts : parts + 3], refs[parts + 3 :]
    wide = groups * piece
    rows = held.shape[1]
    copies = [
        pltpu.make_async_copy(blocks[m], held.at[info[0] ^ m], sems.at[m]) for m in range(parts)
    ]
    for copy in copies:
        copy.start()
    for copy in copies:
        copy.wait()
    for s in range(parts):
        down[s * rows : (s + 1) * rows, :] = held[s, :, 2 * wide :].astype(jnp.float32)
        for target, start in ((gate, 0), (up, wide)):
            for g in range(groups):
                target[:, (g * parts + s) * piece : (g * parts + s + 1) * piece] = held[
                    s, :, start + g * piece : start + (g + 1) * piece
                ].astype(jnp.float32)


def restore(info, blocks, groups, piece):
    parts = len(blocks)
    rows, total = blocks[0].shape
    wide = groups * piece
    whole = pl.BlockSpec(memory_space=pltpu.VMEM)
    return pl.pallas_call(
        functools.partial(restore_kernel, parts, groups, piece),
        out_shape=(
            jax.ShapeDtypeStruct((rows, parts * wide), jnp.float32),
            jax.ShapeDtypeStruct((rows, parts * wide), jnp.float32),
            jax.ShapeDtypeStruct((parts * rows, total - 2 * wide), jnp.float32),
        ),
        in_specs=[pl.BlockSpec(memory_space=pltpu.SMEM)]
        + [pl.BlockSpec(memory_space=pl.ANY)] * parts,
        out_specs=(whole, whole, whole),
        scratch_shapes=[
            pltpu.VMEM((parts, rows, total), jnp.bfloat16),
            pltpu.SemaphoreType.DMA((parts,)),
        ],
        name="restore",
    )(info, *blocks)


def sum_all(array):
    for axis in ("seq", "fsdp"):
        mask = 1
        while mask < lax.axis_size(axis):
            array = array + flip(array, axis, mask)
            mask *= 2
    return array


def total_of(blocks):
    out = blocks[0].astype(jnp.float32)
    for block in blocks[1:]:
        out = out + block.astype(jnp.float32)
    return out


tile = 256
log2e = 1.4426950408889634


def turn(left, right):
    return lax.dot_general(left, right, (((1,), (1,)), ((), ())), preferred_element_type=jnp.float32)


def times(left, right):
    return lax.dot_general(left, right, (((1,), (0,)), ((), ())), preferred_element_type=jnp.float32)


def valid_keys(info, key_tile, size):
    base = (info[0] ^ key_tile) * size
    return lax.broadcasted_iota(jnp.int32, (size, size), 0) < (info[1] - base)


def attend_kernel(heads, info, qkv, out, log_rows, scores):
    seqlen = qkv.shape[0]
    blocks = seqlen // tile
    width = heads * HD
    for h in range(heads):
        value_cols = qkv[:, 2 * width + h * HD : 2 * width + (h + 1) * HD]
        value_turned = value_cols.T

        def one_block(i, carry, h=h, value_turned=value_turned):
            rows = pl.ds(pl.multiple_of(i * tile, tile), tile)
            query = qkv[rows, h * HD : (h + 1) * HD]
            tops = None
            for j in range(blocks):
                keys = qkv[j * tile : (j + 1) * tile, width + h * HD : width + (h + 1) * HD]
                part = jnp.where(valid_keys(info, j, tile), turn(keys, query), -1e30)
                scores[j * tile : (j + 1) * tile, :] = part
                top = jnp.max(part, axis=0, keepdims=True)
                tops = top if tops is None else jnp.maximum(tops, top)
            mixed = None
            total = None
            for j in range(blocks):
                raised = jnp.exp2(
                    (scores[j * tile : (j + 1) * tile, :] - tops) * (log2e * HD ** (-0.5))
                )
                part = jnp.sum(raised, axis=0, keepdims=True)
                total = part if total is None else total + part
                piece = times(
                    value_turned[:, j * tile : (j + 1) * tile], raised.astype(jnp.bfloat16)
                )
                mixed = piece if mixed is None else mixed + piece
            out[rows, h * HD : (h + 1) * HD] = (mixed / total).T.astype(jnp.bfloat16)
            log_rows[h : h + 1, rows] = tops * (log2e * HD ** (-0.5)) + jnp.log2(total)
            return carry

        lax.fori_loop(0, blocks, one_block, 0)


def attend_back_kernel(heads, info, qkv, mixed, grads, log_rows, out, key_sum, value_sum):
    seqlen = qkv.shape[0]
    blocks = seqlen // tile
    width = heads * HD
    scale = HD ** (-0.5)
    for h in range(heads):
        low, high = h * HD, (h + 1) * HD
        key_turned = qkv[:, width + low : width + high].T
        key_sum[...] = jnp.zeros_like(key_sum)
        value_sum[...] = jnp.zeros_like(value_sum)

        def one_block(i, carry, low=low, high=high, h=h, key_turned=key_turned):
            rows = pl.ds(pl.multiple_of(i * tile, tile), tile)
            query = qkv[rows, low:high]
            grad = grads[rows, low:high]
            row_dot = jnp.sum(
                (grad.astype(jnp.float32) * mixed[rows, low:high].astype(jnp.float32)).T,
                axis=0,
                keepdims=True,
            )
            logs = log_rows[h : h + 1, rows]
            query_grad = None
            for j in range(blocks):
                span = slice(j * tile, (j + 1) * tile)
                keys = qkv[span, width + low : width + high]
                values = qkv[span, 2 * width + low : 2 * width + high]
                probs = jnp.where(
                    valid_keys(info, j, tile),
                    jnp.exp2(turn(keys, query) * (log2e * HD ** (-0.5)) - logs),
                    0.0,
                )
                grad_scores = (probs * (turn(values, grad) - row_dot)).astype(jnp.bfloat16)
                value_sum[span, :] += times(probs.astype(jnp.bfloat16), grad)
                key_sum[span, :] += times(grad_scores, query)
                piece = times(key_turned[:, span], grad_scores)
                query_grad = piece if query_grad is None else query_grad + piece
            out[rows, low:high] = (query_grad * scale).T.astype(jnp.bfloat16)
            return carry

        lax.fori_loop(0, blocks, one_block, 0)
        out[:, width + low : width + high] = (key_sum[...] * scale).astype(jnp.bfloat16)
        out[:, 2 * width + low : 2 * width + high] = value_sum[...].astype(jnp.bfloat16)


def attend(info, qkv, heads):
    seqlen = qkv.shape[0]
    whole = pl.BlockSpec(memory_space=pltpu.VMEM)
    return pl.pallas_call(
        functools.partial(attend_kernel, heads),
        out_shape=(
            jax.ShapeDtypeStruct((seqlen, heads * HD), jnp.bfloat16),
            jax.ShapeDtypeStruct((8, seqlen), jnp.float32),
        ),
        in_specs=[pl.BlockSpec(memory_space=pltpu.SMEM), whole],
        out_specs=(whole, whole),
        scratch_shapes=[pltpu.VMEM((seqlen, tile), jnp.float32)],
        cost_estimate=pl.CostEstimate(
            flops=16 * heads * seqlen * seqlen * HD, bytes_accessed=8 * seqlen * heads * HD,
            transcendentals=heads * seqlen * seqlen,
        ),
        name="attend",
    )(info, qkv)


def attend_back(info, qkv, mixed, grads, log_rows, heads):
    seqlen = qkv.shape[0]
    whole = pl.BlockSpec(memory_space=pltpu.VMEM)
    return pl.pallas_call(
        functools.partial(attend_back_kernel, heads),
        out_shape=jax.ShapeDtypeStruct((seqlen, 3 * heads * HD), jnp.bfloat16),
        in_specs=[pl.BlockSpec(memory_space=pltpu.SMEM), whole, whole, whole, whole],
        out_specs=whole,
        scratch_shapes=[
            pltpu.VMEM((seqlen, HD), jnp.float32),
            pltpu.VMEM((seqlen, HD), jnp.float32),
        ],
        cost_estimate=pl.CostEstimate(
            flops=40 * heads * seqlen * seqlen * HD, bytes_accessed=16 * seqlen * heads * HD,
            transcendentals=heads * seqlen * seqlen,
        ),
        name="attend_back",
    )(info, qkv, mixed, grads, log_rows)


def body(
    tokens,
    cotangent,
    w_qkv,
    w_out,
    w_gate,
    w_up,
    w_down,
    gain_one,
    bias_one,
    gain_two,
    bias_two,
    seq_lens,
    slot_seq,
):
    parts = lax.axis_size("seq")
    shards = lax.axis_size("fsdp")
    rank = lax.axis_index("seq")
    owner = lax.axis_index("fsdp")
    rows = tokens.shape[1]
    width = tokens.shape[2]
    shard_rows = w_qkv.shape[0]
    heads = width // HD // parts
    head_width = heads * HD
    hidden = w_down.shape[0]
    piece = hidden // parts
    wide = shards * piece
    seqlen = rows * parts
    stream_in = tokens[0]
    length = lookup(seq_lens, lookup(slot_seq, owner))
    own = jnp.arange(rows, dtype=jnp.int32)
    positions = rank * rows + own
    column = (positions < length).astype(jnp.float32)[:, None]
    block_order = jnp.arange(parts, dtype=jnp.int32) ^ rank
    all_positions = (block_order[:, None] * rows + own[None, :]).reshape(seqlen)
    info = jnp.stack([rank.astype(jnp.int32), length.astype(jnp.int32)])

    stream_blocks = spread(stream_in)
    qkv_piece = lax.dynamic_index_in_dim(
        w_qkv.reshape(shard_rows, 3, parts, head_width), rank, 2, keepdims=False
    ).reshape(shard_rows, 3 * head_width)
    full_qkv, arrived = gather_rows(qkv_piece)
    full_qkv = full_qkv.reshape(width, 3 * head_width)

    def columns_of(weight):
        return lax.dynamic_index_in_dim(
            weight.reshape(shard_rows, shards, parts, piece), rank, 2, keepdims=False
        ).reshape(shard_rows, wide)

    vectors = jnp.concatenate([gain_one, bias_one, gain_two, bias_two])
    vectors = jnp.pad(vectors, (0, width - vectors.shape[0])).reshape(1, width)
    out_piece = jnp.concatenate([w_out, jnp.pad(vectors, ((0, 15), (0, 0)))], axis=0)
    down_piece = lax.dynamic_slice_in_dim(w_down, rank * piece, piece, 0)
    ffn_piece = jnp.concatenate(
        [
            columns_of(w_gate),
            columns_of(w_up),
            down_piece,
        ],
        axis=1,
    )
    out_piece, ffn_piece, arrived = lax.optimization_barrier((out_piece, ffn_piece, arrived))
    gathered_out = gather_rows(out_piece)[0]
    full_out = gathered_out[:, :shard_rows].reshape(width, width)
    params = gathered_out[:, shard_rows, : 4 * shard_rows].astype(jnp.float32)
    params = params.reshape(shards, 4, shard_rows).transpose(1, 0, 2).reshape(4, width)
    gain_first, bias_first, gain_second, bias_second = (params[i : i + 1] for i in range(4))
    full_ffn = gather_rows(ffn_piece)[0].reshape(width, 2 * wide + width)
    full_gate_up = full_ffn[:, : 2 * wide]
    full_down = full_ffn[:, 2 * wide :]

    stream_all = jnp.concatenate(stream_blocks, axis=0)
    projected = jnp.dot(stream_all, full_qkv, preferred_element_type=jnp.float32).reshape(
        seqlen, 3, heads, HD
    )
    cos_table, sin_table = rope_tables(all_positions.astype(jnp.float32), HD)
    cos_table = cos_table[:, None, :]
    sin_table = sin_table[:, None, :]
    queries = rotate(projected[:, 0], cos_table, sin_table).astype(jnp.bfloat16)
    key_rows = rotate(projected[:, 1], cos_table, sin_table).astype(jnp.bfloat16)
    values = projected[:, 2].astype(jnp.bfloat16)
    qkv_rows = jnp.stack([queries, key_rows, values], axis=1).reshape(seqlen, 3 * head_width)
    head_out, log_rows = attend(info, qkv_rows, heads)
    mixed = exchange([head_out[m * rows : (m + 1) * rows] for m in range(parts)])
    head_mix = unmix(mixed, rank).transpose(1, 0, 2).reshape(rows, width)
    branch_attn = jnp.dot(head_mix, full_out, preferred_element_type=jnp.float32)
    stream_float = stream_in.astype(jnp.float32)
    normed_float, normal_one, inverse_one = layer_norm(
        stream_float + branch_attn, gain_first, bias_first
    )
    normed_one = normed_float.astype(jnp.bfloat16)
    normed_all = jnp.concatenate(spread(normed_one), axis=0)
    gate_up = jnp.dot(normed_all, full_gate_up, preferred_element_type=jnp.float32)
    gate_proj = gate_up[:, :wide]
    up_proj = gate_up[:, wide:]
    inner_act = (jax.nn.silu(gate_proj) * up_proj).astype(jnp.bfloat16)
    ffn_part = jnp.dot(inner_act, full_down, preferred_element_type=jnp.float32).astype(
        jnp.bfloat16
    )
    branch_ffn = total_of(exchange([ffn_part[m * rows : (m + 1) * rows] for m in range(parts)]))
    out_float, normal_two, inverse_two = layer_norm(
        normed_one.astype(jnp.float32) + branch_ffn, gain_second, bias_second
    )
    layer_out = (out_float * column).astype(jnp.bfloat16)
    grad_rows = cotangent[0].astype(jnp.float32) * column
    grad_two, gain_two_grad, bias_two_grad = norm_back(
        grad_rows, normal_two, inverse_two, gain_second
    )
    grad_ffn = grad_two.astype(jnp.bfloat16)
    grad_ffn_all = jnp.concatenate(spread(grad_ffn), axis=0)
    grad_inner = jnp.einsum("td,fd->tf", grad_ffn_all, full_down, preferred_element_type=jnp.float32)
    sigmoid_gate = jax.nn.sigmoid(gate_proj)
    grad_gate_rows = (
        grad_inner * up_proj * sigmoid_gate * (1.0 + gate_proj * (1.0 - sigmoid_gate))
    ).astype(jnp.bfloat16)
    grad_up_rows = (grad_inner * gate_proj * sigmoid_gate).astype(jnp.bfloat16)
    grad_both = jnp.concatenate([grad_gate_rows, grad_up_rows], axis=1)
    normed_part = jnp.einsum(
        "tf,df->td", grad_both, full_gate_up, preferred_element_type=jnp.float32
    ).astype(jnp.bfloat16)
    grad_normed = (
        total_of(exchange([normed_part[m * rows : (m + 1) * rows] for m in range(parts)])) + grad_two
    )
    down_grad = jnp.einsum(
        "tf,td->fd", inner_act, grad_ffn_all, preferred_element_type=jnp.float32
    ).astype(jnp.bfloat16)
    both_grad = jnp.einsum(
        "td,tf->df", normed_all, grad_both, preferred_element_type=jnp.float32
    ).astype(jnp.bfloat16)
    ffn_grad = scatter_rows(jnp.concatenate([both_grad, down_grad], axis=1))

    grad_one, gain_one_grad, bias_one_grad = norm_back(
        grad_normed, normal_one, inverse_one, gain_first
    )
    squares = jnp.concatenate(
        [
            jnp.sum(column * stream_float * stream_float, axis=0, keepdims=True),
            jnp.sum(column * branch_attn * branch_attn, axis=0, keepdims=True),
            jnp.sum(column * branch_ffn * branch_ffn, axis=0, keepdims=True),
            gain_one_grad[None],
            bias_one_grad[None],
            gain_two_grad[None],
            bias_two_grad[None],
            jnp.zeros((1, width), jnp.float32),
        ],
        axis=0,
    )
    sums = sum_all(squares)
    denominator = jnp.sum(seq_lens).astype(jnp.float32) * width
    stream_rms = jnp.sqrt(jnp.sum(sums[:3], axis=1) / denominator)
    vector_grads = lax.dynamic_index_in_dim(
        sums[3:7].reshape(4, shards, shard_rows), owner, 1, keepdims=False
    )

    grad_attn = grad_one.astype(jnp.bfloat16)
    grad_mix = (
        jnp.einsum("te,de->td", grad_attn, full_out, preferred_element_type=jnp.float32)
        .astype(jnp.bfloat16)
        .reshape(rows, parts, head_width)
        .transpose(1, 0, 2)
    )
    leaving = [
        lax.dynamic_index_in_dim(grad_mix, rank ^ m, 0, keepdims=False) for m in range(parts)
    ]
    grad_heads = jnp.concatenate(exchange(leaving), axis=0)
    out_grad = scatter_rows(
        jnp.einsum("td,te->de", head_mix, grad_attn, preferred_element_type=jnp.float32).astype(
            jnp.bfloat16
        ),
    )
    grad_qkv = attend_back(info, qkv_rows, head_out, grad_heads, log_rows, heads).reshape(
        seqlen, 3, heads, HD
    )
    grad_proj = jnp.stack(
        [
            unrotate(grad_qkv[:, 0].astype(jnp.float32), cos_table, sin_table),
            unrotate(grad_qkv[:, 1].astype(jnp.float32), cos_table, sin_table),
            grad_qkv[:, 2].astype(jnp.float32),
        ],
        axis=1,
    )
    grad_proj = grad_proj.astype(jnp.bfloat16).reshape(seqlen, 3 * head_width)
    token_part = jnp.einsum(
        "tc,dc->td", grad_proj, full_qkv, preferred_element_type=jnp.float32
    ).astype(jnp.bfloat16)
    grad_tokens = (
        total_of(exchange([token_part[m * rows : (m + 1) * rows] for m in range(parts)])) + grad_one
    ).astype(jnp.bfloat16)
    qkv_grad = scatter_rows(
        jnp.einsum("td,tc->dc", stream_all, grad_proj, preferred_element_type=jnp.float32).astype(
            jnp.bfloat16
        ),
    )
    qkv_blocks = unmix(spread(qkv_grad.astype(jnp.bfloat16)), rank).astype(jnp.float32)
    qkv_out = (
        qkv_blocks.reshape(parts, shard_rows, 3, head_width)
        .transpose(1, 2, 0, 3)
        .reshape(shard_rows, 3 * width)
    )
    ffn_blocks = spread(ffn_grad.astype(jnp.bfloat16))
    if shards <= direct_limit:
        gate_out, up_out, down_out = restore(info, ffn_blocks, shards, piece)
    else:
        ffn_rows = unmix(ffn_blocks, rank).astype(jnp.float32)

        def widen(blocks):
            return (
                blocks.reshape(parts, shard_rows, shards, piece)
                .transpose(1, 2, 0, 3)
                .reshape(shard_rows, shards * hidden)
            )

        gate_out = widen(ffn_rows[:, :, :wide])
        up_out = widen(ffn_rows[:, :, wide : 2 * wide])
        down_out = ffn_rows[:, :, 2 * wide :].reshape(hidden, width)
    out_split = out_grad.astype(jnp.bfloat16).reshape(parts, shard_rows // parts, width)
    out_sum = total_of(
        exchange(
            [lax.dynamic_index_in_dim(out_split, rank ^ m, 0, keepdims=False) for m in range(parts)],
        )
    )
    out_out = (
        unmix(spread(out_sum.astype(jnp.bfloat16)), rank)
        .astype(jnp.float32)
        .reshape(shard_rows, width)
    )
    return (
        layer_out[None],
        grad_tokens[None],
        qkv_out,
        out_out,
        gate_out,
        up_out,
        down_out,
        vector_grads[0],
        vector_grads[1],
        vector_grads[2],
        vector_grads[3],
        stream_rms,
    )


def solution(mesh):
    placed = (
        P("fsdp", "seq", None),
        P("fsdp", "seq", None),
        P("fsdp", None),
        P("fsdp", None),
        P("fsdp", None),
        P("fsdp", None),
        P("fsdp", None),
        P("fsdp"),
        P("fsdp"),
        P("fsdp"),
        P("fsdp"),
        P(),
        P(),
    )

    return jax.shard_map(
        body,
        mesh=mesh,
        in_specs=placed,
        out_specs=(
            P("fsdp", "seq", None),
            P("fsdp", "seq", None),
            P("fsdp", None),
            P("fsdp", None),
            P("fsdp", None),
            P("fsdp", None),
            P("fsdp", None),
            P("fsdp"),
            P("fsdp"),
            P("fsdp"),
            P("fsdp"),
            P(),
        ),
        check_vma=False,
    )
```

```python
import functools

import jax
import jax.numpy as jnp
from jax import lax
from jax.experimental import pallas as pl
from jax.experimental.pallas import tpu as pltpu
from jax.sharding import PartitionSpec as P


HD = 64


epsilon = 1e-12
rope_base = 1000.0
direct_limit = 8


def rope_tables(positions, head_size):
    half_size = head_size // 2
    exponent = jnp.arange(half_size, dtype=jnp.float32) * (2.0 / head_size)
    frequency = jnp.power(jnp.float32(rope_base), -exponent)
    angles = positions[:, None] * frequency[None, :]
    cos_half = jnp.cos(angles)
    sin_half = jnp.sin(angles)
    return (
        jnp.concatenate([cos_half, cos_half], axis=-1),
        jnp.concatenate([sin_half, sin_half], axis=-1),
    )


def rotate(values_in, cos_table, sin_table):
    half_size = values_in.shape[-1] // 2
    turned = jnp.concatenate([-values_in[..., half_size:], values_in[..., :half_size]], axis=-1)
    return values_in * cos_table + turned * sin_table


def lookup(table, position):
    marks = jnp.arange(table.shape[0], dtype=jnp.int32) == position
    return jnp.sum(jnp.where(marks, table, 0))


def layer_norm(stream, gain_vec, bias_vec):
    average = jnp.mean(stream, axis=-1, keepdims=True)
    centred = stream - average
    variance = jnp.mean(centred * centred, axis=-1, keepdims=True)
    inverse = lax.rsqrt(variance + epsilon)
    normal = centred * inverse
    return (normal * gain_vec + bias_vec, normal, inverse)


def norm_back(grad_rows, normal, inverse, gain_vec):
    scaled = grad_rows * gain_vec
    first_mean = jnp.mean(scaled, axis=-1, keepdims=True)
    second_mean = jnp.mean(scaled * normal, axis=-1, keepdims=True)
    grad_in = (scaled - first_mean - normal * second_mean) * inverse
    return (grad_in, jnp.sum(grad_rows * normal, axis=0), jnp.sum(grad_rows, axis=0))


def flip(array, axis, mask):
    count = lax.axis_size(axis)
    return lax.ppermute(array, axis, [(i, i ^ mask) for i in range(count)])


def spread(block):
    return [block] + [flip(block, "seq", m) for m in range(1, lax.axis_size("seq"))]


def exchange(blocks):
    return [blocks[0]] + [flip(blocks[m], "seq", m) for m in range(1, len(blocks))]


def unmix(blocks, rank):
    stacked = jnp.stack(blocks)
    for m, block in enumerate(blocks):
        stacked = lax.dynamic_update_index_in_dim(stacked, block, rank ^ m, 0)
    return stacked


def place_kernel(count, order, *refs):
    out, sems = refs[count], refs[count + 1]
    copies = [
        pltpu.make_async_copy(refs[k], out.at[order[k]], sems.at[k]) for k in range(count)
    ]
    for copy in copies:
        copy.start()
    for copy in copies:
        copy.wait()


def place(blocks, order):
    count = len(blocks)
    shape = blocks[0].shape
    return pl.pallas_call(
        functools.partial(place_kernel, count),
        out_shape=jax.ShapeDtypeStruct((count,) + shape, blocks[0].dtype),
        in_specs=[pl.BlockSpec(memory_space=pltpu.SMEM)]
        + [pl.BlockSpec(memory_space=pl.ANY)] * count,
        out_specs=pl.BlockSpec(memory_space=pltpu.VMEM),
        scratch_shapes=[pltpu.SemaphoreType.DMA((count,))],
        name="place",
    )(order, *blocks)


def gather_rows(shard):
    count = lax.axis_size("fsdp")
    if count > direct_limit:
        return lax.all_gather(shard, "fsdp", axis=0, tiled=False), []
    planes = count // 2
    owner = lax.axis_index("fsdp")
    plane = owner >> 1
    core = owner & 1
    blocks = [shard] + [
        lax.ppermute(shard, "fsdp", [(i, (i + 2 * k) % count) for i in range(count)])
        for k in range(1, planes)
    ]
    swapped = [flip(block, "fsdp", 1) for block in blocks]
    origin = 2 * ((plane - jnp.arange(planes, dtype=jnp.int32)) & (planes - 1))
    order = jnp.concatenate([origin + core, origin + 1 - core])
    return place(blocks + swapped, order), blocks[1:]


def scatter_rows(grad):
    count = lax.axis_size("fsdp")
    if count > direct_limit:
        return lax.psum_scatter(grad, "fsdp", scatter_dimension=0, tiled=True).astype(jnp.float32)
    planes = count // 2
    owner = lax.axis_index("fsdp")
    plane = owner >> 1
    core = owner & 1
    view = grad.reshape(count, grad.shape[0] // count, grad.shape[1])

    def part(k, side):
        place_at = 2 * ((plane + k) & (planes - 1)) + (core ^ side)
        return lax.dynamic_index_in_dim(view, place_at, 0, keepdims=False)

    halves = {}
    for k in list(range(1, planes)) + [0]:
        halves[k] = part(k, 0).astype(jnp.float32) + flip(part(k, 1), "fsdp", 1).astype(jnp.float32)
    total = halves[0]
    for k in range(1, planes):
        total = total + lax.ppermute(
            halves[k].astype(jnp.bfloat16), "fsdp", [(i, (i + 2 * k) % count) for i in range(count)]
        ).astype(jnp.float32)
    return total


def regroup_kernel(groups, size, step, order, source, out, sems):
    per = source.shape[0] // groups
    copies = [
        pltpu.make_async_copy(
            source.at[f, :size],
            out.at[order[f // per], (f % per) * step : (f % per) * step + size],
            sems.at[f],
        )
        for f in range(source.shape[0])
    ]
    for copy in copies:
        copy.start()
    for copy in copies:
        copy.wait()


def regroup(source, order, groups, size):
    count, _, columns = source.shape
    return pl.pallas_call(
        functools.partial(regroup_kernel, groups, size, size),
        out_shape=jax.ShapeDtypeStruct((groups, count // groups * size, columns), source.dtype),
        in_specs=[
            pl.BlockSpec(memory_space=pltpu.SMEM),
            pl.BlockSpec(memory_space=pl.ANY),
        ],
        out_specs=pl.BlockSpec(memory_space=pltpu.VMEM),
        scratch_shapes=[pltpu.SemaphoreType.DMA((count,))],
        name="regroup",
    )(order, source)


def restore_kernel(parts, groups, piece, info, *refs):
    blocks, (gate, up, down), (held, sems) = refs[:parts], refs[parts : parts + 3], refs[parts + 3 :]
    wide = groups * piece
    rows = held.shape[1]
    copies = [
        pltpu.make_async_copy(blocks[m], held.at[info[0] ^ m], sems.at[m]) for m in range(parts)
    ]
    for copy in copies:
        copy.start()
    for copy in copies:
        copy.wait()
    for s in range(parts):
        down[s * rows : (s + 1) * rows, :] = held[s, :, 2 * wide :].astype(jnp.float32)
        for target, start in ((gate, 0), (up, wide)):
            for g in range(groups):
                target[:, (g * parts + s) * piece : (g * parts + s + 1) * piece] = held[
                    s, :, start + g * piece : start + (g + 1) * piece
                ].astype(jnp.float32)


def restore(info, blocks, groups, piece):
    parts = len(blocks)
    rows, total = blocks[0].shape
    wide = groups * piece
    whole = pl.BlockSpec(memory_space=pltpu.VMEM)
    return pl.pallas_call(
        functools.partial(restore_kernel, parts, groups, piece),
        out_shape=(
            jax.ShapeDtypeStruct((rows, parts * wide), jnp.float32),
            jax.ShapeDtypeStruct((rows, parts * wide), jnp.float32),
            jax.ShapeDtypeStruct((parts * rows, total - 2 * wide), jnp.float32),
        ),
        in_specs=[pl.BlockSpec(memory_space=pltpu.SMEM)]
        + [pl.BlockSpec(memory_space=pl.ANY)] * parts,
        out_specs=(whole, whole, whole),
        scratch_shapes=[
            pltpu.VMEM((parts, rows, total), jnp.bfloat16),
            pltpu.SemaphoreType.DMA((parts,)),
        ],
        name="restore",
    )(info, *blocks)


def total_of(blocks):
    out = blocks[0].astype(jnp.float32)
    for block in blocks[1:]:
        out = out + block.astype(jnp.float32)
    return out


tile = 256
log2e = 1.4426950408889634


def turn(left, right):
    return lax.dot_general(left, right, (((1,), (1,)), ((), ())), preferred_element_type=jnp.float32)


def times(left, right):
    return lax.dot_general(left, right, (((1,), (0,)), ((), ())), preferred_element_type=jnp.float32)


def valid_keys(info, key_tile, size):
    base = (info[0] ^ key_tile) * size
    return lax.broadcasted_iota(jnp.int32, (size, size), 0) < (info[1] - base)


def attend_kernel(heads, info, qkv, out, log_rows, scores):
    seqlen = qkv.shape[0]
    blocks = seqlen // tile
    width = heads * HD
    for h in range(heads):
        value_cols = qkv[:, 2 * width + h * HD : 2 * width + (h + 1) * HD]
        value_turned = value_cols.T

        def one_block(i, carry, h=h, value_turned=value_turned):
            rows = pl.ds(pl.multiple_of(i * tile, tile), tile)
            query = qkv[rows, h * HD : (h + 1) * HD]
            tops = None
            for j in range(blocks):
                keys = qkv[j * tile : (j + 1) * tile, width + h * HD : width + (h + 1) * HD]
                part = jnp.where(valid_keys(info, j, tile), turn(keys, query), -1e30)
                scores[j * tile : (j + 1) * tile, :] = part
                top = jnp.max(part, axis=0, keepdims=True)
                tops = top if tops is None else jnp.maximum(tops, top)
            mixed = None
            total = None
            for j in range(blocks):
                raised = jnp.exp2(
                    (scores[j * tile : (j + 1) * tile, :] - tops) * (log2e * HD ** (-0.5))
                )
                part = jnp.sum(raised, axis=0, keepdims=True)
                total = part if total is None else total + part
                piece = times(
                    value_turned[:, j * tile : (j + 1) * tile], raised.astype(jnp.bfloat16)
                )
                mixed = piece if mixed is None else mixed + piece
            out[rows, h * HD : (h + 1) * HD] = (mixed / total).T.astype(jnp.bfloat16)
            log_rows[h : h + 1, rows] = tops * (log2e * HD ** (-0.5)) + jnp.log2(total)
            return carry

        lax.fori_loop(0, blocks, one_block, 0)


def unturn(turned, turns):
    half = HD // 2
    cos, sin = turns[:half], turns[half:]
    first, second = turned[:half], turned[half:]
    return jnp.concatenate([first * cos + second * sin, second * cos - first * sin], axis=0)


def attend_back_kernel(heads, info, qkv, mixed, grads, log_rows, turns, out, key_sum, value_sum):
    seqlen = qkv.shape[0]
    blocks = seqlen // tile
    width = heads * HD
    scale = HD ** (-0.5)
    for h in range(heads):
        low, high = h * HD, (h + 1) * HD
        key_turned = qkv[:, width + low : width + high].T
        key_sum[...] = jnp.zeros_like(key_sum)
        value_sum[...] = jnp.zeros_like(value_sum)

        def one_block(i, carry, low=low, high=high, h=h, key_turned=key_turned):
            rows = pl.ds(pl.multiple_of(i * tile, tile), tile)
            query = qkv[rows, low:high]
            grad = grads[rows, low:high]
            row_dot = jnp.sum(
                (grad.astype(jnp.float32) * mixed[rows, low:high].astype(jnp.float32)).T,
                axis=0,
                keepdims=True,
            )
            logs = log_rows[h : h + 1, rows]
            query_grad = None
            for j in range(blocks):
                span = slice(j * tile, (j + 1) * tile)
                keys = qkv[span, width + low : width + high]
                values = qkv[span, 2 * width + low : 2 * width + high]
                probs = jnp.where(
                    valid_keys(info, j, tile),
                    jnp.exp2(turn(keys, query) * (log2e * HD ** (-0.5)) - logs),
                    0.0,
                )
                grad_scores = (probs * (turn(values, grad) - row_dot)).astype(jnp.bfloat16)
                value_sum[span, :] += times(probs.astype(jnp.bfloat16), grad)
                key_sum[span, :] += times(grad_scores, query)
                piece = times(key_turned[:, span], grad_scores)
                query_grad = piece if query_grad is None else query_grad + piece
            out[rows, low:high] = unturn(query_grad * scale, turns[:, rows]).T.astype(jnp.bfloat16)
            return carry

        lax.fori_loop(0, blocks, one_block, 0)
        key_grad = unturn((key_sum[...] * scale).T, turns[...]).T
        out[:, width + low : width + high] = key_grad.astype(jnp.bfloat16)
        out[:, 2 * width + low : 2 * width + high] = value_sum[...].astype(jnp.bfloat16)


def attend(info, qkv, heads):
    seqlen = qkv.shape[0]
    whole = pl.BlockSpec(memory_space=pltpu.VMEM)
    return pl.pallas_call(
        functools.partial(attend_kernel, heads),
        out_shape=(
            jax.ShapeDtypeStruct((seqlen, heads * HD), jnp.bfloat16),
            jax.ShapeDtypeStruct((8, seqlen), jnp.float32),
        ),
        in_specs=[pl.BlockSpec(memory_space=pltpu.SMEM), whole],
        out_specs=(whole, whole),
        scratch_shapes=[pltpu.VMEM((seqlen, tile), jnp.float32)],
        cost_estimate=pl.CostEstimate(
            flops=16 * heads * seqlen * seqlen * HD, bytes_accessed=8 * seqlen * heads * HD,
            transcendentals=heads * seqlen * seqlen,
        ),
        name="attend",
    )(info, qkv)


def attend_back(info, qkv, mixed, grads, log_rows, turns, heads):
    seqlen = qkv.shape[0]
    whole = pl.BlockSpec(memory_space=pltpu.VMEM)
    return pl.pallas_call(
        functools.partial(attend_back_kernel, heads),
        out_shape=jax.ShapeDtypeStruct((seqlen, 3 * heads * HD), jnp.bfloat16),
        in_specs=[pl.BlockSpec(memory_space=pltpu.SMEM)] + [whole] * 5,
        out_specs=whole,
        scratch_shapes=[
            pltpu.VMEM((seqlen, HD), jnp.float32),
            pltpu.VMEM((seqlen, HD), jnp.float32),
        ],
        cost_estimate=pl.CostEstimate(
            flops=40 * heads * seqlen * seqlen * HD, bytes_accessed=16 * seqlen * heads * HD,
            transcendentals=heads * seqlen * seqlen,
        ),
        name="attend_back",
    )(info, qkv, mixed, grads, log_rows, turns)


def body(
    tokens,
    cotangent,
    w_qkv,
    w_out,
    w_gate,
    w_up,
    w_down,
    gain_one,
    bias_one,
    gain_two,
    bias_two,
    seq_lens,
    slot_seq,
):
    parts = lax.axis_size("seq")
    shards = lax.axis_size("fsdp")
    rank = lax.axis_index("seq")
    owner = lax.axis_index("fsdp")
    rows = tokens.shape[1]
    width = tokens.shape[2]
    shard_rows = w_qkv.shape[0]
    heads = width // HD // parts
    head_width = heads * HD
    hidden = w_down.shape[0]
    piece = hidden // parts
    wide = shards * piece
    seqlen = rows * parts
    stream_in = tokens[0]
    length = lookup(seq_lens, lookup(slot_seq, owner))
    own = jnp.arange(rows, dtype=jnp.int32)
    positions = rank * rows + own
    column = (positions < length).astype(jnp.float32)[:, None]
    block_order = jnp.arange(parts, dtype=jnp.int32) ^ rank
    all_positions = (block_order[:, None] * rows + own[None, :]).reshape(seqlen)
    info = jnp.stack([rank.astype(jnp.int32), length.astype(jnp.int32)])

    stream_blocks = spread(stream_in)
    qkv_piece = lax.dynamic_index_in_dim(
        w_qkv.reshape(shard_rows, 3, parts, head_width), rank, 2, keepdims=False
    ).reshape(shard_rows, 3 * head_width)
    full_qkv, arrived = gather_rows(qkv_piece)
    full_qkv = full_qkv.reshape(width, 3 * head_width)

    def columns_of(weight):
        return lax.dynamic_index_in_dim(
            weight.reshape(shard_rows, shards, parts, piece), rank, 2, keepdims=False
        ).reshape(shard_rows, wide)

    vectors = jnp.concatenate([gain_one, bias_one, gain_two, bias_two])
    vectors = jnp.pad(vectors, (0, width - vectors.shape[0])).reshape(1, width)
    out_piece = jnp.concatenate([w_out, jnp.pad(vectors, ((0, 15), (0, 0)))], axis=0)
    down_piece = lax.dynamic_slice_in_dim(w_down, rank * piece, piece, 0)
    ffn_piece = jnp.concatenate(
        [
            columns_of(w_gate),
            columns_of(w_up),
            down_piece,
        ],
        axis=1,
    )
    out_piece, ffn_piece, arrived = lax.optimization_barrier((out_piece, ffn_piece, arrived))
    gathered_out = lax.all_gather(out_piece, "fsdp", axis=0, tiled=False)
    if shards <= direct_limit:
        full_out = regroup(gathered_out, block_order, parts, shard_rows).reshape(width, width)
    else:
        full_out = jnp.take(
            gathered_out[:, :shard_rows].reshape(parts, head_width, width), block_order, axis=0
        ).reshape(width, width)
    params = gathered_out[:, shard_rows, : 4 * shard_rows].astype(jnp.float32)
    params = params.reshape(shards, 4, shard_rows).transpose(1, 0, 2).reshape(4, width)
    gain_first, bias_first, gain_second, bias_second = (params[i : i + 1] for i in range(4))
    full_ffn = lax.all_gather(ffn_piece, "fsdp", axis=0, tiled=True)
    full_gate_up = full_ffn[:, : 2 * wide]
    full_down = full_ffn[:, 2 * wide :]

    stream_all = jnp.concatenate(stream_blocks, axis=0)
    projected = jnp.dot(stream_all, full_qkv, preferred_element_type=jnp.float32).reshape(
        seqlen, 3, heads, HD
    )
    cos_table, sin_table = rope_tables(all_positions.astype(jnp.float32), HD)
    turns = jnp.concatenate([cos_table[:, : HD // 2].T, sin_table[:, : HD // 2].T], axis=0)
    cos_table = cos_table[:, None, :]
    sin_table = sin_table[:, None, :]
    queries = rotate(projected[:, 0], cos_table, sin_table).astype(jnp.bfloat16)
    key_rows = rotate(projected[:, 1], cos_table, sin_table).astype(jnp.bfloat16)
    values = projected[:, 2].astype(jnp.bfloat16)
    qkv_rows = jnp.stack([queries, key_rows, values], axis=1).reshape(seqlen, 3 * head_width)
    head_out, log_rows = attend(info, qkv_rows, heads)
    mixed = exchange([head_out[m * rows : (m + 1) * rows] for m in range(parts)])
    head_mix = jnp.concatenate(mixed, axis=1)
    branch_attn = jnp.dot(head_mix, full_out, preferred_element_type=jnp.float32)
    stream_float = stream_in.astype(jnp.float32)
    normed_float, normal_one, inverse_one = layer_norm(
        stream_float + branch_attn, gain_first, bias_first
    )
    normed_one = normed_float.astype(jnp.bfloat16)
    normed_all = jnp.concatenate(spread(normed_one), axis=0)
    gate_up = jnp.dot(normed_all, full_gate_up, preferred_element_type=jnp.float32)
    gate_proj = gate_up[:, :wide]
    up_proj = gate_up[:, wide:]
    inner_act = (jax.nn.silu(gate_proj) * up_proj).astype(jnp.bfloat16)
    ffn_part = jnp.dot(inner_act, full_down, preferred_element_type=jnp.float32).astype(
        jnp.bfloat16
    )
    branch_ffn = total_of(exchange([ffn_part[m * rows : (m + 1) * rows] for m in range(parts)]))
    out_float, normal_two, inverse_two = layer_norm(
        normed_one.astype(jnp.float32) + branch_ffn, gain_second, bias_second
    )
    layer_out = (out_float * column).astype(jnp.bfloat16)
    grad_rows = cotangent[0].astype(jnp.float32) * column
    grad_two, gain_two_grad, bias_two_grad = norm_back(
        grad_rows, normal_two, inverse_two, gain_second
    )
    grad_ffn = grad_two.astype(jnp.bfloat16)
    grad_ffn_all = jnp.concatenate(spread(grad_ffn), axis=0)
    grad_inner = jnp.einsum("td,fd->tf", grad_ffn_all, full_down, preferred_element_type=jnp.float32)
    sigmoid_gate = jax.nn.sigmoid(gate_proj)
    grad_gate_rows = (
        grad_inner * up_proj * sigmoid_gate * (1.0 + gate_proj * (1.0 - sigmoid_gate))
    ).astype(jnp.bfloat16)
    grad_up_rows = (grad_inner * gate_proj * sigmoid_gate).astype(jnp.bfloat16)
    grad_both = jnp.concatenate([grad_gate_rows, grad_up_rows], axis=1)
    normed_part = jnp.einsum(
        "tf,df->td", grad_both, full_gate_up, preferred_element_type=jnp.float32
    ).astype(jnp.bfloat16)
    grad_normed = (
        total_of(exchange([normed_part[m * rows : (m + 1) * rows] for m in range(parts)])) + grad_two
    )
    down_grad = jnp.einsum(
        "tf,td->fd", inner_act, grad_ffn_all, preferred_element_type=jnp.float32
    ).astype(jnp.bfloat16)
    both_grad = jnp.einsum(
        "td,tf->df", normed_all, grad_both, preferred_element_type=jnp.float32
    ).astype(jnp.bfloat16)
    ffn_grad = lax.psum_scatter(
        jnp.concatenate([both_grad, down_grad], axis=1),
        "fsdp",
        scatter_dimension=0,
        tiled=True,
    )

    grad_one, gain_one_grad, bias_one_grad = norm_back(
        grad_normed, normal_one, inverse_one, gain_first
    )
    grad_attn = grad_one.astype(jnp.bfloat16)
    grad_mix = jnp.einsum(
        "te,de->td", grad_attn, full_out, preferred_element_type=jnp.float32
    ).astype(jnp.bfloat16)
    leaving = [grad_mix[:, m * head_width : (m + 1) * head_width] for m in range(parts)]
    grad_heads = jnp.concatenate(exchange(leaving), axis=0)
    out_part = jnp.einsum(
        "td,te->de", head_mix, grad_attn, preferred_element_type=jnp.float32
    ).astype(jnp.bfloat16)
    if shards <= direct_limit:
        out_part = regroup(out_part.reshape(parts, head_width, width), block_order, parts, head_width)
    else:
        out_part = jnp.take(out_part.reshape(parts, head_width, width), block_order, axis=0)
    vectors_part = (
        jnp.stack([gain_one_grad, bias_one_grad, gain_two_grad, bias_two_grad])
        .reshape(4, shards, shard_rows)
        .transpose(1, 0, 2)
        .reshape(shards, 1, 4 * shard_rows)
    )
    vectors_part = jnp.pad(vectors_part, ((0, 0), (0, 0), (0, width - 4 * shard_rows)))
    squares = jnp.stack(
        [
            jnp.sum(column * stream_float * stream_float, axis=0),
            jnp.sum(column * branch_attn * branch_attn, axis=0),
            jnp.sum(column * branch_ffn * branch_ffn, axis=0),
        ]
    )
    squares = jnp.broadcast_to(squares[None], (shards, 3, width))
    extra_part = jnp.concatenate(
        [vectors_part, squares, jnp.zeros((shards, 12, width), jnp.float32)], axis=1
    ).astype(jnp.bfloat16)
    out_grad = lax.psum_scatter(
        jnp.concatenate([out_part.reshape(shards, shard_rows, width), extra_part], axis=1),
        "fsdp",
        scatter_dimension=0,
        tiled=True,
    )[0]
    out_blocks = [block.astype(jnp.float32) for block in spread(out_grad)]
    while len(out_blocks) > 1:
        out_blocks = [
            out_blocks[i] + out_blocks[i + 1] for i in range(0, len(out_blocks), 2)
        ]
    out_out = out_blocks[0][:shard_rows]
    vector_grads = out_blocks[0][shard_rows, : 4 * shard_rows].reshape(4, shard_rows)
    denominator = jnp.sum(seq_lens).astype(jnp.float32) * width
    stream_rms = jnp.sqrt(
        jnp.sum(out_blocks[0][shard_rows + 1 : shard_rows + 4], axis=1) / denominator
    )
    grad_proj = attend_back(info, qkv_rows, head_out, grad_heads, log_rows, turns, heads)
    token_part = jnp.einsum(
        "tc,dc->td", grad_proj, full_qkv, preferred_element_type=jnp.float32
    ).astype(jnp.bfloat16)
    grad_tokens = (
        total_of(exchange([token_part[m * rows : (m + 1) * rows] for m in range(parts)])) + grad_one
    ).astype(jnp.bfloat16)
    qkv_grad = scatter_rows(
        jnp.einsum("td,tc->dc", stream_all, grad_proj, preferred_element_type=jnp.float32).astype(
            jnp.bfloat16
        ),
    )
    qkv_blocks = unmix(spread(qkv_grad.astype(jnp.bfloat16)), rank).astype(jnp.float32)
    qkv_out = (
        qkv_blocks.reshape(parts, shard_rows, 3, head_width)
        .transpose(1, 2, 0, 3)
        .reshape(shard_rows, 3 * width)
    )
    ffn_blocks = spread(ffn_grad.astype(jnp.bfloat16))
    if shards <= direct_limit:
        gate_out, up_out, down_out = restore(info, ffn_blocks, shards, piece)
    else:
        ffn_rows = unmix(ffn_blocks, rank).astype(jnp.float32)

        def widen(blocks):
            return (
                blocks.reshape(parts, shard_rows, shards, piece)
                .transpose(1, 2, 0, 3)
                .reshape(shard_rows, shards * hidden)
            )

        gate_out = widen(ffn_rows[:, :, :wide])
        up_out = widen(ffn_rows[:, :, wide : 2 * wide])
        down_out = ffn_rows[:, :, 2 * wide :].reshape(hidden, width)
    return (
        layer_out[None],
        grad_tokens[None],
        qkv_out,
        out_out,
        gate_out,
        up_out,
        down_out,
        vector_grads[0],
        vector_grads[1],
        vector_grads[2],
        vector_grads[3],
        stream_rms,
    )


def solution(mesh):
    placed = (
        P("fsdp", "seq", None),
        P("fsdp", "seq", None),
        P("fsdp", None),
        P("fsdp", None),
        P("fsdp", None),
        P("fsdp", None),
        P("fsdp", None),
        P("fsdp"),
        P("fsdp"),
        P("fsdp"),
        P("fsdp"),
        P(),
        P(),
    )

    return jax.shard_map(
        body,
        mesh=mesh,
        in_specs=placed,
        out_specs=(
            P("fsdp", "seq", None),
            P("fsdp", "seq", None),
            P("fsdp", None),
            P("fsdp", None),
            P("fsdp", None),
            P("fsdp", None),
            P("fsdp", None),
            P("fsdp"),
            P("fsdp"),
            P("fsdp"),
            P("fsdp"),
            P(),
        ),
        check_vma=False,
    )
```

```python
import functools

import jax
import jax.numpy as jnp
from jax import lax
from jax.experimental import pallas as pl
from jax.experimental.pallas import tpu as pltpu
from jax.sharding import PartitionSpec as P


HD = 64


epsilon = 1e-12
rope_base = 1000.0
direct_limit = 8


def rope_tables(positions, head_size):
    half_size = head_size // 2
    exponent = jnp.arange(half_size, dtype=jnp.float32) * (2.0 / head_size)
    frequency = jnp.power(jnp.float32(rope_base), -exponent)
    angles = positions[:, None] * frequency[None, :]
    cos_half = jnp.cos(angles)
    sin_half = jnp.sin(angles)
    return (
        jnp.concatenate([cos_half, cos_half], axis=-1),
        jnp.concatenate([sin_half, sin_half], axis=-1),
    )


def rotate(values_in, cos_table, sin_table):
    half_size = values_in.shape[-1] // 2
    turned = jnp.concatenate([-values_in[..., half_size:], values_in[..., :half_size]], axis=-1)
    return values_in * cos_table + turned * sin_table


def lookup(table, position):
    marks = jnp.arange(table.shape[0], dtype=jnp.int32) == position
    return jnp.sum(jnp.where(marks, table, 0))


def layer_norm(stream, gain_vec, bias_vec):
    average = jnp.mean(stream, axis=-1, keepdims=True)
    centred = stream - average
    variance = jnp.mean(centred * centred, axis=-1, keepdims=True)
    inverse = lax.rsqrt(variance + epsilon)
    normal = centred * inverse
    return (normal * gain_vec + bias_vec, normal, inverse)


def norm_back(grad_rows, normal, inverse, gain_vec):
    scaled = grad_rows * gain_vec
    first_mean = jnp.mean(scaled, axis=-1, keepdims=True)
    second_mean = jnp.mean(scaled * normal, axis=-1, keepdims=True)
    grad_in = (scaled - first_mean - normal * second_mean) * inverse
    return (grad_in, jnp.sum(grad_rows * normal, axis=0), jnp.sum(grad_rows, axis=0))


def flip(array, axis, mask):
    count = lax.axis_size(axis)
    return lax.ppermute(array, axis, [(i, i ^ mask) for i in range(count)])


def spread(block):
    return [block] + [flip(block, "seq", m) for m in range(1, lax.axis_size("seq"))]


def exchange(blocks):
    return [blocks[0]] + [flip(blocks[m], "seq", m) for m in range(1, len(blocks))]


def unmix(blocks, rank):
    stacked = jnp.stack(blocks)
    for m, block in enumerate(blocks):
        stacked = lax.dynamic_update_index_in_dim(stacked, block, rank ^ m, 0)
    return stacked


def place_kernel(count, order, *refs):
    out, sems = refs[count], refs[count + 1]
    copies = [
        pltpu.make_async_copy(refs[k], out.at[order[k]], sems.at[k]) for k in range(count)
    ]
    for copy in copies:
        copy.start()
    for copy in copies:
        copy.wait()


def place(blocks, order):
    count = len(blocks)
    shape = blocks[0].shape
    return pl.pallas_call(
        functools.partial(place_kernel, count),
        out_shape=jax.ShapeDtypeStruct((count,) + shape, blocks[0].dtype),
        in_specs=[pl.BlockSpec(memory_space=pltpu.SMEM)]
        + [pl.BlockSpec(memory_space=pl.ANY)] * count,
        out_specs=pl.BlockSpec(memory_space=pltpu.VMEM),
        scratch_shapes=[pltpu.SemaphoreType.DMA((count,))],
        name="place",
    )(order, *blocks)


def gather_rows(shard):
    count = lax.axis_size("fsdp")
    if count > direct_limit:
        return lax.all_gather(shard, "fsdp", axis=0, tiled=False), []
    planes = count // 2
    owner = lax.axis_index("fsdp")
    plane = owner >> 1
    core = owner & 1
    blocks = [shard] + [
        lax.ppermute(shard, "fsdp", [(i, (i + 2 * k) % count) for i in range(count)])
        for k in range(1, planes)
    ]
    swapped = [flip(block, "fsdp", 1) for block in blocks]
    origin = 2 * ((plane - jnp.arange(planes, dtype=jnp.int32)) & (planes - 1))
    order = jnp.concatenate([origin + core, origin + 1 - core])
    return place(blocks + swapped, order), blocks[1:]


def scatter_rows(grad):
    count = lax.axis_size("fsdp")
    if count > direct_limit:
        return lax.psum_scatter(grad, "fsdp", scatter_dimension=0, tiled=True).astype(jnp.float32)
    planes = count // 2
    owner = lax.axis_index("fsdp")
    plane = owner >> 1
    core = owner & 1
    view = grad.reshape(count, grad.shape[0] // count, grad.shape[1])

    def part(k, side):
        place_at = 2 * ((plane + k) & (planes - 1)) + (core ^ side)
        return lax.dynamic_index_in_dim(view, place_at, 0, keepdims=False)

    halves = {}
    for k in list(range(1, planes)) + [0]:
        halves[k] = part(k, 0).astype(jnp.float32) + flip(part(k, 1), "fsdp", 1).astype(jnp.float32)
    total = halves[0]
    for k in range(1, planes):
        total = total + lax.ppermute(
            halves[k].astype(jnp.bfloat16), "fsdp", [(i, (i + 2 * k) % count) for i in range(count)]
        ).astype(jnp.float32)
    return total


def regroup_kernel(groups, size, step, order, source, out, sems):
    per = source.shape[0] // groups
    copies = [
        pltpu.make_async_copy(
            source.at[f, :size],
            out.at[order[f // per], (f % per) * step : (f % per) * step + size],
            sems.at[f],
        )
        for f in range(source.shape[0])
    ]
    for copy in copies:
        copy.start()
    for copy in copies:
        copy.wait()


def regroup(source, order, groups, size):
    count, _, columns = source.shape
    return pl.pallas_call(
        functools.partial(regroup_kernel, groups, size, size),
        out_shape=jax.ShapeDtypeStruct((groups, count // groups * size, columns), source.dtype),
        in_specs=[
            pl.BlockSpec(memory_space=pltpu.SMEM),
            pl.BlockSpec(memory_space=pl.ANY),
        ],
        out_specs=pl.BlockSpec(memory_space=pltpu.VMEM),
        scratch_shapes=[pltpu.SemaphoreType.DMA((count,))],
        name="regroup",
    )(order, source)


def restore_kernel(parts, groups, piece, info, *refs):
    blocks, (gate, up, down), (held, sems) = refs[:parts], refs[parts : parts + 3], refs[parts + 3 :]
    wide = groups * piece
    rows = held.shape[1]
    copies = [
        pltpu.make_async_copy(blocks[m], held.at[info[0] ^ m], sems.at[m]) for m in range(parts)
    ]
    for copy in copies:
        copy.start()
    for copy in copies:
        copy.wait()
    for s in range(parts):
        down[s * rows : (s + 1) * rows, :] = held[s, :, 2 * wide :].astype(jnp.float32)
        for target, start in ((gate, 0), (up, wide)):
            for g in range(groups):
                target[:, (g * parts + s) * piece : (g * parts + s + 1) * piece] = held[
                    s, :, start + g * piece : start + (g + 1) * piece
                ].astype(jnp.float32)


def restore(info, blocks, groups, piece):
    parts = len(blocks)
    rows, total = blocks[0].shape
    wide = groups * piece
    whole = pl.BlockSpec(memory_space=pltpu.VMEM)
    return pl.pallas_call(
        functools.partial(restore_kernel, parts, groups, piece),
        out_shape=(
            jax.ShapeDtypeStruct((rows, parts * wide), jnp.float32),
            jax.ShapeDtypeStruct((rows, parts * wide), jnp.float32),
            jax.ShapeDtypeStruct((parts * rows, total - 2 * wide), jnp.float32),
        ),
        in_specs=[pl.BlockSpec(memory_space=pltpu.SMEM)]
        + [pl.BlockSpec(memory_space=pl.ANY)] * parts,
        out_specs=(whole, whole, whole),
        scratch_shapes=[
            pltpu.VMEM((parts, rows, total), jnp.bfloat16),
            pltpu.SemaphoreType.DMA((parts,)),
        ],
        name="restore",
    )(info, *blocks)


def total_of(blocks):
    out = blocks[0].astype(jnp.float32)
    for block in blocks[1:]:
        out = out + block.astype(jnp.float32)
    return out


tile = 256
log2e = 1.4426950408889634


def turn(left, right):
    return lax.dot_general(left, right, (((1,), (1,)), ((), ())), preferred_element_type=jnp.float32)


def times(left, right):
    return lax.dot_general(left, right, (((1,), (0,)), ((), ())), preferred_element_type=jnp.float32)


def valid_keys(info, key_tile, size):
    base = (info[0] ^ key_tile) * size
    return lax.broadcasted_iota(jnp.int32, (size, size), 0) < (info[1] - base)


def attend_kernel(heads, info, qkv, out, log_rows, scores):
    seqlen = qkv.shape[0]
    blocks = seqlen // tile
    width = heads * HD
    for h in range(heads):
        value_cols = qkv[:, 2 * width + h * HD : 2 * width + (h + 1) * HD]
        value_turned = value_cols.T

        def one_block(i, carry, h=h, value_turned=value_turned):
            rows = pl.ds(pl.multiple_of(i * tile, tile), tile)
            query = qkv[rows, h * HD : (h + 1) * HD]
            tops = None
            for j in range(blocks):
                keys = qkv[j * tile : (j + 1) * tile, width + h * HD : width + (h + 1) * HD]
                part = jnp.where(valid_keys(info, j, tile), turn(keys, query), -1e30)
                scores[j * tile : (j + 1) * tile, :] = part
                top = jnp.max(part, axis=0, keepdims=True)
                tops = top if tops is None else jnp.maximum(tops, top)
            mixed = None
            total = None
            for j in range(blocks):
                raised = jnp.exp2(
                    (scores[j * tile : (j + 1) * tile, :] - tops) * (log2e * HD ** (-0.5))
                )
                part = jnp.sum(raised, axis=0, keepdims=True)
                total = part if total is None else total + part
                piece = times(
                    value_turned[:, j * tile : (j + 1) * tile], raised.astype(jnp.bfloat16)
                )
                mixed = piece if mixed is None else mixed + piece
            out[rows, h * HD : (h + 1) * HD] = (mixed / total).T.astype(jnp.bfloat16)
            log_rows[h : h + 1, rows] = tops * (log2e * HD ** (-0.5)) + jnp.log2(total)
            return carry

        lax.fori_loop(0, blocks, one_block, 0)


def unturn(turned, turns):
    half = HD // 2
    cos, sin = turns[:half], turns[half:]
    first, second = turned[:half], turned[half:]
    return jnp.concatenate([first * cos + second * sin, second * cos - first * sin], axis=0)


def attend_back_kernel(heads, chosen, info, qkv, mixed, grads, log_rows, turns, *refs):
    out, key_sum, value_sum = refs[-3:]
    seqlen = qkv.shape[0]
    blocks = seqlen // tile
    width = heads * HD
    scale = HD ** (-0.5)
    step = out.shape[1] // 3
    shift = chosen[0] if step < width else 0
    if len(refs) > 3:
        known = refs[0].shape[1] // 3
        for part in range(3):
            out[:, part * step : part * step + known] = refs[0][
                :, part * known : (part + 1) * known
            ]
    for h in chosen:
        low, high = h * HD, (h + 1) * HD
        left, right = low - shift * HD, high - shift * HD
        key_turned = qkv[:, width + low : width + high].T
        key_sum[...] = jnp.zeros_like(key_sum)
        value_sum[...] = jnp.zeros_like(value_sum)

        def one_block(i, carry, low=low, high=high, h=h, left=left, right=right, key_turned=key_turned):
            rows = pl.ds(pl.multiple_of(i * tile, tile), tile)
            query = qkv[rows, low:high]
            grad = grads[rows, low:high]
            row_dot = jnp.sum(
                (grad.astype(jnp.float32) * mixed[rows, low:high].astype(jnp.float32)).T,
                axis=0,
                keepdims=True,
            )
            logs = log_rows[h : h + 1, rows]
            query_grad = None
            for j in range(blocks):
                span = slice(j * tile, (j + 1) * tile)
                keys = qkv[span, width + low : width + high]
                values = qkv[span, 2 * width + low : 2 * width + high]
                probs = jnp.where(
                    valid_keys(info, j, tile),
                    jnp.exp2(turn(keys, query) * (log2e * HD ** (-0.5)) - logs),
                    0.0,
                )
                grad_scores = (probs * (turn(values, grad) - row_dot)).astype(jnp.bfloat16)
                value_sum[span, :] += times(probs.astype(jnp.bfloat16), grad)
                key_sum[span, :] += times(grad_scores, query)
                piece = times(key_turned[:, span], grad_scores)
                query_grad = piece if query_grad is None else query_grad + piece
            out[rows, left:right] = unturn(query_grad * scale, turns[:, rows]).T.astype(jnp.bfloat16)
            return carry

        lax.fori_loop(0, blocks, one_block, 0)
        key_grad = unturn((key_sum[...] * scale).T, turns[...]).T
        out[:, step + left : step + right] = key_grad.astype(jnp.bfloat16)
        out[:, 2 * step + left : 2 * step + right] = value_sum[...].astype(jnp.bfloat16)


def attend(info, qkv, heads):
    seqlen = qkv.shape[0]
    whole = pl.BlockSpec(memory_space=pltpu.VMEM)
    return pl.pallas_call(
        functools.partial(attend_kernel, heads),
        out_shape=(
            jax.ShapeDtypeStruct((seqlen, heads * HD), jnp.bfloat16),
            jax.ShapeDtypeStruct((8, seqlen), jnp.float32),
        ),
        in_specs=[pl.BlockSpec(memory_space=pltpu.SMEM), whole],
        out_specs=(whole, whole),
        scratch_shapes=[pltpu.VMEM((seqlen, tile), jnp.float32)],
        cost_estimate=pl.CostEstimate(
            flops=16 * heads * seqlen * seqlen * HD, bytes_accessed=8 * seqlen * heads * HD,
            transcendentals=heads * seqlen * seqlen,
        ),
        name="attend",
    )(info, qkv)


def attend_back(info, qkv, mixed, grads, log_rows, turns, heads, chosen, known):
    seqlen = qkv.shape[0]
    whole = pl.BlockSpec(memory_space=pltpu.VMEM)
    count = heads if known else len(chosen)
    return pl.pallas_call(
        functools.partial(attend_back_kernel, heads, chosen),
        out_shape=jax.ShapeDtypeStruct((seqlen, 3 * count * HD), jnp.bfloat16),
        in_specs=[pl.BlockSpec(memory_space=pltpu.SMEM)] + [whole] * (5 + len(known)),
        out_specs=whole,
        scratch_shapes=[
            pltpu.VMEM((seqlen, HD), jnp.float32),
            pltpu.VMEM((seqlen, HD), jnp.float32),
        ],
        cost_estimate=pl.CostEstimate(
            flops=40 * len(chosen) * seqlen * seqlen * HD,
            bytes_accessed=16 * seqlen * heads * HD,
            transcendentals=len(chosen) * seqlen * seqlen,
        ),
    )(info, qkv, mixed, grads, log_rows, turns, *known)


def body(
    tokens,
    cotangent,
    w_qkv,
    w_out,
    w_gate,
    w_up,
    w_down,
    gain_one,
    bias_one,
    gain_two,
    bias_two,
    seq_lens,
    slot_seq,
):
    parts = lax.axis_size("seq")
    shards = lax.axis_size("fsdp")
    rank = lax.axis_index("seq")
    owner = lax.axis_index("fsdp")
    rows = tokens.shape[1]
    width = tokens.shape[2]
    shard_rows = w_qkv.shape[0]
    heads = width // HD // parts
    head_width = heads * HD
    hidden = w_down.shape[0]
    piece = hidden // parts
    wide = shards * piece
    seqlen = rows * parts
    stream_in = tokens[0]
    length = lookup(seq_lens, lookup(slot_seq, owner))
    own = jnp.arange(rows, dtype=jnp.int32)
    positions = rank * rows + own
    column = (positions < length).astype(jnp.float32)[:, None]
    block_order = jnp.arange(parts, dtype=jnp.int32) ^ rank
    all_positions = (block_order[:, None] * rows + own[None, :]).reshape(seqlen)
    info = jnp.stack([rank.astype(jnp.int32), length.astype(jnp.int32)])

    stream_blocks = spread(stream_in)
    qkv_piece = lax.dynamic_index_in_dim(
        w_qkv.reshape(shard_rows, 3, parts, head_width), rank, 2, keepdims=False
    ).reshape(shard_rows, 3 * head_width)
    full_qkv, arrived = gather_rows(qkv_piece)
    full_qkv = full_qkv.reshape(width, 3 * head_width)

    def columns_of(weight):
        return lax.dynamic_index_in_dim(
            weight.reshape(shard_rows, shards, parts, piece), rank, 2, keepdims=False
        ).reshape(shard_rows, wide)

    vectors = jnp.concatenate([gain_one, bias_one, gain_two, bias_two])
    vectors = jnp.pad(vectors, (0, width - vectors.shape[0])).reshape(1, width)
    out_piece = jnp.concatenate([w_out, jnp.pad(vectors, ((0, 15), (0, 0)))], axis=0)
    down_piece = lax.dynamic_slice_in_dim(w_down, rank * piece, piece, 0)
    ffn_piece = jnp.concatenate(
        [
            columns_of(w_gate),
            columns_of(w_up),
            down_piece,
        ],
        axis=1,
    )
    out_piece, ffn_piece, arrived = lax.optimization_barrier((out_piece, ffn_piece, arrived))
    gathered_out = lax.all_gather(out_piece, "fsdp", axis=0, tiled=False)
    if shards <= direct_limit:
        full_out = regroup(gathered_out, block_order, parts, shard_rows).reshape(width, width)
    else:
        full_out = jnp.take(
            gathered_out[:, :shard_rows].reshape(parts, head_width, width), block_order, axis=0
        ).reshape(width, width)
    params = gathered_out[:, shard_rows, : 4 * shard_rows].astype(jnp.float32)
    params = params.reshape(shards, 4, shard_rows).transpose(1, 0, 2).reshape(4, width)
    gain_first, bias_first, gain_second, bias_second = (params[i : i + 1] for i in range(4))
    full_ffn = lax.all_gather(ffn_piece, "fsdp", axis=0, tiled=True)
    full_gate_up = full_ffn[:, : 2 * wide]
    full_down = full_ffn[:, 2 * wide :]

    stream_all = jnp.concatenate(stream_blocks, axis=0)
    projected = jnp.dot(stream_all, full_qkv, preferred_element_type=jnp.float32).reshape(
        seqlen, 3, heads, HD
    )
    cos_table, sin_table = rope_tables(all_positions.astype(jnp.float32), HD)
    turns = jnp.concatenate([cos_table[:, : HD // 2].T, sin_table[:, : HD // 2].T], axis=0)
    cos_table = cos_table[:, None, :]
    sin_table = sin_table[:, None, :]
    queries = rotate(projected[:, 0], cos_table, sin_table).astype(jnp.bfloat16)
    key_rows = rotate(projected[:, 1], cos_table, sin_table).astype(jnp.bfloat16)
    values = projected[:, 2].astype(jnp.bfloat16)
    qkv_rows = jnp.stack([queries, key_rows, values], axis=1).reshape(seqlen, 3 * head_width)
    head_out, log_rows = attend(info, qkv_rows, heads)
    mixed = exchange([head_out[m * rows : (m + 1) * rows] for m in range(parts)])
    head_mix = jnp.concatenate(mixed, axis=1)
    branch_attn = jnp.dot(head_mix, full_out, preferred_element_type=jnp.float32)
    stream_float = stream_in.astype(jnp.float32)
    normed_float, normal_one, inverse_one = layer_norm(
        stream_float + branch_attn, gain_first, bias_first
    )
    normed_one = normed_float.astype(jnp.bfloat16)
    normed_blocks = spread(normed_one)
    gates, ups, inners, ffn_parts = [], [], [], []
    for block in normed_blocks:
        gate_up = jnp.dot(block, full_gate_up, preferred_element_type=jnp.float32)
        gates.append(gate_up[:, :wide])
        ups.append(gate_up[:, wide:])
        inners.append((jax.nn.silu(gates[-1]) * ups[-1]).astype(jnp.bfloat16))
        ffn_parts.append(
            jnp.dot(inners[-1], full_down, preferred_element_type=jnp.float32).astype(jnp.bfloat16)
        )
    normed_all = jnp.concatenate(normed_blocks, axis=0)
    inner_act = jnp.concatenate(inners, axis=0)
    branch_ffn = total_of(exchange(ffn_parts))
    out_float, normal_two, inverse_two = layer_norm(
        normed_one.astype(jnp.float32) + branch_ffn, gain_second, bias_second
    )
    layer_out = (out_float * column).astype(jnp.bfloat16)
    grad_rows = cotangent[0].astype(jnp.float32) * column
    grad_two, gain_two_grad, bias_two_grad = norm_back(
        grad_rows, normal_two, inverse_two, gain_second
    )
    grad_ffn = grad_two.astype(jnp.bfloat16)
    grad_blocks = spread(grad_ffn)
    grad_boths, normed_parts = [], []
    for block, gate_proj, up_proj in zip(grad_blocks, gates, ups):
        grad_inner = jnp.einsum("td,fd->tf", block, full_down, preferred_element_type=jnp.float32)
        sigmoid_gate = jax.nn.sigmoid(gate_proj)
        grad_gate_rows = (
            grad_inner * up_proj * sigmoid_gate * (1.0 + gate_proj * (1.0 - sigmoid_gate))
        ).astype(jnp.bfloat16)
        grad_up_rows = (grad_inner * gate_proj * sigmoid_gate).astype(jnp.bfloat16)
        grad_boths.append(jnp.concatenate([grad_gate_rows, grad_up_rows], axis=1))
        normed_parts.append(
            jnp.einsum(
                "tf,df->td", grad_boths[-1], full_gate_up, preferred_element_type=jnp.float32
            ).astype(jnp.bfloat16)
        )
    grad_ffn_all = jnp.concatenate(grad_blocks, axis=0)
    grad_both = jnp.concatenate(grad_boths, axis=0)
    grad_normed = total_of(exchange(normed_parts)) + grad_two
    down_grad = jnp.einsum(
        "tf,td->fd", inner_act, grad_ffn_all, preferred_element_type=jnp.float32
    ).astype(jnp.bfloat16)
    both_grad = jnp.einsum(
        "td,tf->df", normed_all, grad_both, preferred_element_type=jnp.float32
    ).astype(jnp.bfloat16)
    ffn_grad = lax.psum_scatter(
        jnp.concatenate([both_grad, down_grad], axis=1),
        "fsdp",
        scatter_dimension=0,
        tiled=True,
    )

    grad_one, gain_one_grad, bias_one_grad = norm_back(
        grad_normed, normal_one, inverse_one, gain_first
    )
    grad_attn = grad_one.astype(jnp.bfloat16)
    grad_mix = jnp.einsum(
        "te,de->td", grad_attn, full_out, preferred_element_type=jnp.float32
    ).astype(jnp.bfloat16)
    leaving = [grad_mix[:, m * head_width : (m + 1) * head_width] for m in range(parts)]
    grad_heads = jnp.concatenate(exchange(leaving), axis=0)
    out_part = jnp.einsum(
        "td,te->de", head_mix, grad_attn, preferred_element_type=jnp.float32
    ).astype(jnp.bfloat16)
    if shards <= direct_limit:
        out_part = regroup(out_part.reshape(parts, head_width, width), block_order, parts, head_width)
    else:
        out_part = jnp.take(out_part.reshape(parts, head_width, width), block_order, axis=0)
    vectors_part = (
        jnp.stack([gain_one_grad, bias_one_grad, gain_two_grad, bias_two_grad])
        .reshape(4, shards, shard_rows)
        .transpose(1, 0, 2)
        .reshape(shards, 1, 4 * shard_rows)
    )
    vectors_part = jnp.pad(vectors_part, ((0, 0), (0, 0), (0, width - 4 * shard_rows)))
    squares = jnp.stack(
        [
            jnp.sum(column * stream_float * stream_float, axis=0),
            jnp.sum(column * branch_attn * branch_attn, axis=0),
            jnp.sum(column * branch_ffn * branch_ffn, axis=0),
        ]
    )
    squares = jnp.broadcast_to(squares[None], (shards, 3, width))
    extra_part = jnp.concatenate(
        [vectors_part, squares, jnp.zeros((shards, 12, width), jnp.float32)], axis=1
    ).astype(jnp.bfloat16)
    out_grad = lax.psum_scatter(
        jnp.concatenate([out_part.reshape(shards, shard_rows, width), extra_part], axis=1),
        "fsdp",
        scatter_dimension=0,
        tiled=True,
    )[0]
    out_blocks = [block.astype(jnp.float32) for block in spread(out_grad)]
    while len(out_blocks) > 1:
        out_blocks = [
            out_blocks[i] + out_blocks[i + 1] for i in range(0, len(out_blocks), 2)
        ]
    out_out = out_blocks[0][:shard_rows]
    vector_grads = out_blocks[0][shard_rows, : 4 * shard_rows].reshape(4, shard_rows)
    denominator = jnp.sum(seq_lens).astype(jnp.float32) * width
    stream_rms = jnp.sqrt(
        jnp.sum(out_blocks[0][shard_rows + 1 : shard_rows + 4], axis=1) / denominator
    )
    back_args = (info, qkv_rows, head_out, grad_heads, log_rows, turns, heads)
    first_part = attend_back(*back_args, tuple(range(1)), ())
    grad_proj = attend_back(*back_args, tuple(range(1, heads)), (first_part,))
    token_parts = [
        jnp.einsum(
            "tc,dc->td",
            grad_proj[m * rows : (m + 1) * rows],
            full_qkv,
            preferred_element_type=jnp.float32,
        ).astype(jnp.bfloat16)
        for m in range(parts)
    ]
    grad_tokens = (total_of(exchange(token_parts)) + grad_one).astype(jnp.bfloat16)
    qkv_grad = scatter_rows(
        jnp.einsum("td,tc->dc", stream_all, grad_proj, preferred_element_type=jnp.float32).astype(
            jnp.bfloat16
        ),
    )
    qkv_blocks = unmix(spread(qkv_grad.astype(jnp.bfloat16)), rank).astype(jnp.float32)
    qkv_out = (
        qkv_blocks.reshape(parts, shard_rows, 3, head_width)
        .transpose(1, 2, 0, 3)
        .reshape(shard_rows, 3 * width)
    )
    ffn_blocks = spread(ffn_grad.astype(jnp.bfloat16))
    if shards <= direct_limit:
        gate_out, up_out, down_out = restore(info, ffn_blocks, shards, piece)
    else:
        ffn_rows = unmix(ffn_blocks, rank).astype(jnp.float32)

        def widen(blocks):
            return (
                blocks.reshape(parts, shard_rows, shards, piece)
                .transpose(1, 2, 0, 3)
                .reshape(shard_rows, shards * hidden)
            )

        gate_out = widen(ffn_rows[:, :, :wide])
        up_out = widen(ffn_rows[:, :, wide : 2 * wide])
        down_out = ffn_rows[:, :, 2 * wide :].reshape(hidden, width)
    return (
        layer_out[None],
        grad_tokens[None],
        qkv_out,
        out_out,
        gate_out,
        up_out,
        down_out,
        vector_grads[0],
        vector_grads[1],
        vector_grads[2],
        vector_grads[3],
        stream_rms,
    )


def solution(mesh):
    placed = (
        P("fsdp", "seq", None),
        P("fsdp", "seq", None),
        P("fsdp", None),
        P("fsdp", None),
        P("fsdp", None),
        P("fsdp", None),
        P("fsdp", None),
        P("fsdp"),
        P("fsdp"),
        P("fsdp"),
        P("fsdp"),
        P(),
        P(),
    )

    return jax.shard_map(
        body,
        mesh=mesh,
        in_specs=placed,
        out_specs=(
            P("fsdp", "seq", None),
            P("fsdp", "seq", None),
            P("fsdp", None),
            P("fsdp", None),
            P("fsdp", None),
            P("fsdp", None),
            P("fsdp", None),
            P("fsdp"),
            P("fsdp"),
            P("fsdp"),
            P("fsdp"),
            P(),
        ),
        check_vma=False,
    )
```

```python
import functools

import jax
import jax.numpy as jnp
from jax import lax
from jax.experimental import pallas as pl
from jax.experimental.pallas import tpu as pltpu
from jax.sharding import PartitionSpec as P


HD = 64


epsilon = 1e-12
rope_base = 1000.0
direct_limit = 8


def rope_tables(positions, head_size):
    half_size = head_size // 2
    exponent = jnp.arange(half_size, dtype=jnp.float32) * (2.0 / head_size)
    frequency = jnp.power(jnp.float32(rope_base), -exponent)
    angles = positions[:, None] * frequency[None, :]
    cos_half = jnp.cos(angles)
    sin_half = jnp.sin(angles)
    return (
        jnp.concatenate([cos_half, cos_half], axis=-1),
        jnp.concatenate([sin_half, sin_half], axis=-1),
    )


def rotate(values_in, cos_table, sin_table):
    half_size = values_in.shape[-1] // 2
    turned = jnp.concatenate([-values_in[..., half_size:], values_in[..., :half_size]], axis=-1)
    return values_in * cos_table + turned * sin_table


def lookup(table, position):
    marks = jnp.arange(table.shape[0], dtype=jnp.int32) == position
    return jnp.sum(jnp.where(marks, table, 0))


def layer_norm(stream, gain_vec, bias_vec):
    average = jnp.mean(stream, axis=-1, keepdims=True)
    centred = stream - average
    variance = jnp.mean(centred * centred, axis=-1, keepdims=True)
    inverse = lax.rsqrt(variance + epsilon)
    normal = centred * inverse
    return (normal * gain_vec + bias_vec, normal, inverse)


def norm_back(grad_rows, normal, inverse, gain_vec):
    scaled = grad_rows * gain_vec
    first_mean = jnp.mean(scaled, axis=-1, keepdims=True)
    second_mean = jnp.mean(scaled * normal, axis=-1, keepdims=True)
    grad_in = (scaled - first_mean - normal * second_mean) * inverse
    return (grad_in, jnp.sum(grad_rows * normal, axis=0), jnp.sum(grad_rows, axis=0))


def flip(array, axis, mask):
    count = lax.axis_size(axis)
    return lax.ppermute(array, axis, [(i, i ^ mask) for i in range(count)])


def spread(block):
    return [block] + [flip(block, "seq", m) for m in range(1, lax.axis_size("seq"))]


def exchange(blocks):
    return [blocks[0]] + [flip(blocks[m], "seq", m) for m in range(1, len(blocks))]


def unmix(blocks, rank):
    stacked = jnp.stack(blocks)
    for m, block in enumerate(blocks):
        stacked = lax.dynamic_update_index_in_dim(stacked, block, rank ^ m, 0)
    return stacked


def place_kernel(count, order, *refs):
    out, sems = refs[count], refs[count + 1]
    copies = [
        pltpu.make_async_copy(refs[k], out.at[order[k]], sems.at[k]) for k in range(count)
    ]
    for copy in copies:
        copy.start()
    for copy in copies:
        copy.wait()


def place(blocks, order):
    count = len(blocks)
    shape = blocks[0].shape
    return pl.pallas_call(
        functools.partial(place_kernel, count),
        out_shape=jax.ShapeDtypeStruct((count,) + shape, blocks[0].dtype),
        in_specs=[pl.BlockSpec(memory_space=pltpu.SMEM)]
        + [pl.BlockSpec(memory_space=pl.ANY)] * count,
        out_specs=pl.BlockSpec(memory_space=pltpu.VMEM),
        scratch_shapes=[pltpu.SemaphoreType.DMA((count,))],
        name="place",
    )(order, *blocks)


def gather_rows(shard):
    count = lax.axis_size("fsdp")
    if count > direct_limit:
        return lax.all_gather(shard, "fsdp", axis=0, tiled=False)
    planes = count // 2
    owner = lax.axis_index("fsdp")
    plane = owner >> 1
    core = owner & 1
    blocks = [shard] + [
        lax.ppermute(shard, "fsdp", [(i, (i + 2 * k) % count) for i in range(count)])
        for k in range(1, planes)
    ]
    swapped = [flip(block, "fsdp", 1) for block in blocks]
    origin = 2 * ((plane - jnp.arange(planes, dtype=jnp.int32)) & (planes - 1))
    order = jnp.concatenate([origin + core, origin + 1 - core])
    return place(blocks + swapped, order)


def scatter_rows(grad):
    count = lax.axis_size("fsdp")
    if count > direct_limit:
        return lax.psum_scatter(grad, "fsdp", scatter_dimension=0, tiled=True).astype(jnp.float32)
    planes = count // 2
    owner = lax.axis_index("fsdp")
    plane = owner >> 1
    core = owner & 1
    view = grad.reshape(count, grad.shape[0] // count, grad.shape[1])

    def part(k, side):
        place_at = 2 * ((plane + k) & (planes - 1)) + (core ^ side)
        return lax.dynamic_index_in_dim(view, place_at, 0, keepdims=False)

    halves = {}
    for k in list(range(1, planes)) + [0]:
        halves[k] = part(k, 0).astype(jnp.float32) + flip(part(k, 1), "fsdp", 1).astype(jnp.float32)
    total = halves[0]
    for k in range(1, planes):
        total = total + lax.ppermute(
            halves[k].astype(jnp.bfloat16), "fsdp", [(i, (i + 2 * k) % count) for i in range(count)]
        ).astype(jnp.float32)
    return total


def regroup_kernel(groups, size, step, order, source, out, sems):
    per = source.shape[0] // groups
    copies = [
        pltpu.make_async_copy(
            source.at[f, :size],
            out.at[order[f // per], (f % per) * step : (f % per) * step + size],
            sems.at[f],
        )
        for f in range(source.shape[0])
    ]
    for copy in copies:
        copy.start()
    for copy in copies:
        copy.wait()


def regroup(source, order, groups, size):
    count, _, columns = source.shape
    return pl.pallas_call(
        functools.partial(regroup_kernel, groups, size, size),
        out_shape=jax.ShapeDtypeStruct((groups, count // groups * size, columns), source.dtype),
        in_specs=[
            pl.BlockSpec(memory_space=pltpu.SMEM),
            pl.BlockSpec(memory_space=pl.ANY),
        ],
        out_specs=pl.BlockSpec(memory_space=pltpu.VMEM),
        scratch_shapes=[pltpu.SemaphoreType.DMA((count,))],
        name="regroup",
    )(order, source)


def restore_kernel(parts, groups, piece, info, *refs):
    blocks, (gate, up, down), (held, sems) = refs[:parts], refs[parts : parts + 3], refs[parts + 3 :]
    wide = groups * piece
    rows = held.shape[1]
    copies = [
        pltpu.make_async_copy(blocks[m], held.at[info[0] ^ m], sems.at[m]) for m in range(parts)
    ]
    for copy in copies:
        copy.start()
    for copy in copies:
        copy.wait()
    for s in range(parts):
        down[s * rows : (s + 1) * rows, :] = held[s, :, 2 * wide :].astype(jnp.float32)
        for target, start in ((gate, 0), (up, wide)):
            for g in range(groups):
                target[:, (g * parts + s) * piece : (g * parts + s + 1) * piece] = held[
                    s, :, start + g * piece : start + (g + 1) * piece
                ].astype(jnp.float32)


def restore(info, blocks, groups, piece):
    parts = len(blocks)
    rows, total = blocks[0].shape
    wide = groups * piece
    whole = pl.BlockSpec(memory_space=pltpu.VMEM)
    return pl.pallas_call(
        functools.partial(restore_kernel, parts, groups, piece),
        out_shape=(
            jax.ShapeDtypeStruct((rows, parts * wide), jnp.float32),
            jax.ShapeDtypeStruct((rows, parts * wide), jnp.float32),
            jax.ShapeDtypeStruct((parts * rows, total - 2 * wide), jnp.float32),
        ),
        in_specs=[pl.BlockSpec(memory_space=pltpu.SMEM)]
        + [pl.BlockSpec(memory_space=pl.ANY)] * parts,
        out_specs=(whole, whole, whole),
        scratch_shapes=[
            pltpu.VMEM((parts, rows, total), jnp.bfloat16),
            pltpu.SemaphoreType.DMA((parts,)),
        ],
        name="restore",
    )(info, *blocks)


def total_of(blocks):
    out = blocks[0].astype(jnp.float32)
    for block in blocks[1:]:
        out = out + block.astype(jnp.float32)
    return out


tile = 256
log2e = 1.4426950408889634


def turn(left, right):
    return lax.dot_general(left, right, (((1,), (1,)), ((), ())), preferred_element_type=jnp.float32)


def times(left, right):
    return lax.dot_general(left, right, (((1,), (0,)), ((), ())), preferred_element_type=jnp.float32)


def valid_keys(info, key_tile, size):
    base = (info[0] ^ key_tile) * size
    return lax.broadcasted_iota(jnp.int32, (size, size), 0) < (info[1] - base)


def attend_kernel(heads, info, qkv, out, log_rows, scores):
    seqlen = qkv.shape[0]
    blocks = seqlen // tile
    width = heads * HD
    for h in range(heads):
        value_cols = qkv[:, 2 * width + h * HD : 2 * width + (h + 1) * HD]
        value_turned = value_cols.T

        def one_block(i, carry, h=h, value_turned=value_turned):
            rows = pl.ds(pl.multiple_of(i * tile, tile), tile)
            query = qkv[rows, h * HD : (h + 1) * HD]
            tops = None
            for j in range(blocks):
                keys = qkv[j * tile : (j + 1) * tile, width + h * HD : width + (h + 1) * HD]
                part = jnp.where(valid_keys(info, j, tile), turn(keys, query), -1e30)
                scores[j * tile : (j + 1) * tile, :] = part
                top = jnp.max(part, axis=0, keepdims=True)
                tops = top if tops is None else jnp.maximum(tops, top)
            mixed = None
            total = None
            for j in range(blocks):
                raised = jnp.exp2(
                    (scores[j * tile : (j + 1) * tile, :] - tops) * (log2e * HD ** (-0.5))
                )
                part = jnp.sum(raised, axis=0, keepdims=True)
                total = part if total is None else total + part
                piece = times(
                    value_turned[:, j * tile : (j + 1) * tile], raised.astype(jnp.bfloat16)
                )
                mixed = piece if mixed is None else mixed + piece
            out[rows, h * HD : (h + 1) * HD] = (mixed / total).T.astype(jnp.bfloat16)
            log_rows[h : h + 1, rows] = tops * (log2e * HD ** (-0.5)) + jnp.log2(total)
            return carry

        lax.fori_loop(0, blocks, one_block, 0)


def unturn(turned, turns):
    half = HD // 2
    cos, sin = turns[:half], turns[half:]
    first, second = turned[:half], turned[half:]
    return jnp.concatenate([first * cos + second * sin, second * cos - first * sin], axis=0)


def attend_back_kernel(heads, chosen, info, qkv, mixed, grads, log_rows, turns, *refs):
    out, key_sum, value_sum = refs[-3:]
    seqlen = qkv.shape[0]
    blocks = seqlen // tile
    width = heads * HD
    scale = HD ** (-0.5)
    step = out.shape[1] // 3
    shift = chosen[0] if step < width else 0
    if len(refs) > 3:
        known = refs[0].shape[1] // 3
        for part in range(3):
            out[:, part * step : part * step + known] = refs[0][
                :, part * known : (part + 1) * known
            ]
    for h in chosen:
        low, high = h * HD, (h + 1) * HD
        left, right = low - shift * HD, high - shift * HD
        key_turned = qkv[:, width + low : width + high].T
        key_sum[...] = jnp.zeros_like(key_sum)
        value_sum[...] = jnp.zeros_like(value_sum)

        def one_block(i, carry, low=low, high=high, h=h, left=left, right=right, key_turned=key_turned):
            rows = pl.ds(pl.multiple_of(i * tile, tile), tile)
            query = qkv[rows, low:high]
            grad = grads[rows, low:high]
            row_dot = jnp.sum(
                (grad.astype(jnp.float32) * mixed[rows, low:high].astype(jnp.float32)).T,
                axis=0,
                keepdims=True,
            )
            logs = log_rows[h : h + 1, rows]
            query_grad = None
            for j in range(blocks):
                span = slice(j * tile, (j + 1) * tile)
                keys = qkv[span, width + low : width + high]
                values = qkv[span, 2 * width + low : 2 * width + high]
                probs = jnp.where(
                    valid_keys(info, j, tile),
                    jnp.exp2(turn(keys, query) * (log2e * HD ** (-0.5)) - logs),
                    0.0,
                )
                grad_scores = (probs * (turn(values, grad) - row_dot)).astype(jnp.bfloat16)
                value_sum[span, :] += times(probs.astype(jnp.bfloat16), grad)
                key_sum[span, :] += times(grad_scores, query)
                piece = times(key_turned[:, span], grad_scores)
                query_grad = piece if query_grad is None else query_grad + piece
            out[rows, left:right] = unturn(query_grad * scale, turns[:, rows]).T.astype(jnp.bfloat16)
            return carry

        lax.fori_loop(0, blocks, one_block, 0)
        key_grad = unturn((key_sum[...] * scale).T, turns[...]).T
        out[:, step + left : step + right] = key_grad.astype(jnp.bfloat16)
        out[:, 2 * step + left : 2 * step + right] = value_sum[...].astype(jnp.bfloat16)


def attend(info, qkv, heads):
    seqlen = qkv.shape[0]
    whole = pl.BlockSpec(memory_space=pltpu.VMEM)
    return pl.pallas_call(
        functools.partial(attend_kernel, heads),
        out_shape=(
            jax.ShapeDtypeStruct((seqlen, heads * HD), jnp.bfloat16),
            jax.ShapeDtypeStruct((8, seqlen), jnp.float32),
        ),
        in_specs=[pl.BlockSpec(memory_space=pltpu.SMEM), whole],
        out_specs=(whole, whole),
        scratch_shapes=[pltpu.VMEM((seqlen, tile), jnp.float32)],
        cost_estimate=pl.CostEstimate(
            flops=16 * heads * seqlen * seqlen * HD, bytes_accessed=8 * seqlen * heads * HD,
            transcendentals=heads * seqlen * seqlen,
        ),
        name="attend",
    )(info, qkv)


def attend_back(info, qkv, mixed, grads, log_rows, turns, heads, chosen, known):
    seqlen = qkv.shape[0]
    whole = pl.BlockSpec(memory_space=pltpu.VMEM)
    count = heads if known else len(chosen)
    return pl.pallas_call(
        functools.partial(attend_back_kernel, heads, chosen),
        out_shape=jax.ShapeDtypeStruct((seqlen, 3 * count * HD), jnp.bfloat16),
        in_specs=[pl.BlockSpec(memory_space=pltpu.SMEM)] + [whole] * (5 + len(known)),
        out_specs=whole,
        scratch_shapes=[
            pltpu.VMEM((seqlen, HD), jnp.float32),
            pltpu.VMEM((seqlen, HD), jnp.float32),
        ],
        cost_estimate=pl.CostEstimate(
            flops=40 * len(chosen) * seqlen * seqlen * HD,
            bytes_accessed=16 * seqlen * heads * HD,
            transcendentals=len(chosen) * seqlen * seqlen,
        ),
    )(info, qkv, mixed, grads, log_rows, turns, *known)


def body(
    tokens,
    cotangent,
    w_qkv,
    w_out,
    w_gate,
    w_up,
    w_down,
    gain_one,
    bias_one,
    gain_two,
    bias_two,
    seq_lens,
    slot_seq,
):
    parts = lax.axis_size("seq")
    shards = lax.axis_size("fsdp")
    rank = lax.axis_index("seq")
    owner = lax.axis_index("fsdp")
    rows = tokens.shape[1]
    width = tokens.shape[2]
    shard_rows = w_qkv.shape[0]
    heads = width // HD // parts
    head_width = heads * HD
    hidden = w_down.shape[0]
    piece = hidden // parts
    wide = shards * piece
    seqlen = rows * parts
    stream_in = tokens[0]
    length = lookup(seq_lens, lookup(slot_seq, owner))
    own = jnp.arange(rows, dtype=jnp.int32)
    positions = rank * rows + own
    column = (positions < length).astype(jnp.float32)[:, None]
    block_order = jnp.arange(parts, dtype=jnp.int32) ^ rank
    all_positions = (block_order[:, None] * rows + own[None, :]).reshape(seqlen)
    info = jnp.stack([rank.astype(jnp.int32), length.astype(jnp.int32)])

    stream_blocks = spread(stream_in)
    qkv_piece = lax.dynamic_index_in_dim(
        w_qkv.reshape(shard_rows, 3, parts, head_width), rank, 2, keepdims=False
    ).reshape(shard_rows, 3 * head_width)
    full_qkv = gather_rows(qkv_piece).reshape(width, 3 * head_width)

    def columns_of(weight):
        return lax.dynamic_index_in_dim(
            weight.reshape(shard_rows, shards, parts, piece), rank, 2, keepdims=False
        ).reshape(shard_rows, wide)

    vectors = jnp.concatenate([gain_one, bias_one, gain_two, bias_two])
    vectors = jnp.pad(vectors, (0, width - vectors.shape[0])).reshape(1, width)
    out_piece = jnp.concatenate([w_out, jnp.pad(vectors, ((0, 15), (0, 0)))], axis=0)
    down_piece = lax.dynamic_slice_in_dim(w_down, rank * piece, piece, 0)
    ffn_piece = jnp.concatenate(
        [
            columns_of(w_gate),
            columns_of(w_up),
            down_piece,
        ],
        axis=1,
    )
    gathered_out = lax.all_gather(out_piece, "fsdp", axis=0, tiled=False)
    if shards <= direct_limit:
        full_out = regroup(gathered_out, block_order, parts, shard_rows).reshape(width, width)
    else:
        full_out = jnp.take(
            gathered_out[:, :shard_rows].reshape(parts, head_width, width), block_order, axis=0
        ).reshape(width, width)
    params = gathered_out[:, shard_rows, : 4 * shard_rows].astype(jnp.float32)
    params = params.reshape(shards, 4, shard_rows).transpose(1, 0, 2).reshape(4, width)
    gain_first, bias_first, gain_second, bias_second = (params[i : i + 1] for i in range(4))
    full_ffn = lax.all_gather(ffn_piece, "fsdp", axis=0, tiled=True)
    full_gate_up = full_ffn[:, : 2 * wide]
    full_down = full_ffn[:, 2 * wide :]

    stream_all = jnp.concatenate(stream_blocks, axis=0)
    projected = jnp.dot(stream_all, full_qkv, preferred_element_type=jnp.float32).reshape(
        seqlen, 3, heads, HD
    )
    cos_table, sin_table = rope_tables(all_positions.astype(jnp.float32), HD)
    turns = jnp.concatenate([cos_table[:, : HD // 2].T, sin_table[:, : HD // 2].T], axis=0)
    cos_table = cos_table[:, None, :]
    sin_table = sin_table[:, None, :]
    queries = rotate(projected[:, 0], cos_table, sin_table).astype(jnp.bfloat16)
    key_rows = rotate(projected[:, 1], cos_table, sin_table).astype(jnp.bfloat16)
    values = projected[:, 2].astype(jnp.bfloat16)
    qkv_rows = jnp.stack([queries, key_rows, values], axis=1).reshape(seqlen, 3 * head_width)
    head_out, log_rows = attend(info, qkv_rows, heads)
    mixed = exchange([head_out[m * rows : (m + 1) * rows] for m in range(parts)])
    head_mix = jnp.concatenate(mixed, axis=1)
    branch_attn = jnp.dot(head_mix, full_out, preferred_element_type=jnp.float32)
    stream_float = stream_in.astype(jnp.float32)
    normed_float, normal_one, inverse_one = layer_norm(
        stream_float + branch_attn, gain_first, bias_first
    )
    normed_one = normed_float.astype(jnp.bfloat16)
    normed_blocks = spread(normed_one)
    gates, ups, inners, ffn_parts = [], [], [], []
    for block in normed_blocks:
        gate_up = jnp.dot(block, full_gate_up, preferred_element_type=jnp.float32)
        gates.append(gate_up[:, :wide])
        ups.append(gate_up[:, wide:])
        inners.append((jax.nn.silu(gates[-1]) * ups[-1]).astype(jnp.bfloat16))
        ffn_parts.append(
            jnp.dot(inners[-1], full_down, preferred_element_type=jnp.float32).astype(jnp.bfloat16)
        )
    normed_all = jnp.concatenate(normed_blocks, axis=0)
    inner_act = jnp.concatenate(inners, axis=0)
    branch_ffn = total_of(exchange(ffn_parts))
    out_float, normal_two, inverse_two = layer_norm(
        normed_one.astype(jnp.float32) + branch_ffn, gain_second, bias_second
    )
    layer_out = (out_float * column).astype(jnp.bfloat16)
    grad_rows = cotangent[0].astype(jnp.float32) * column
    grad_two, gain_two_grad, bias_two_grad = norm_back(
        grad_rows, normal_two, inverse_two, gain_second
    )
    grad_ffn = grad_two.astype(jnp.bfloat16)
    grad_blocks = spread(grad_ffn)
    grad_boths, normed_parts = [], []
    for block, gate_proj, up_proj in zip(grad_blocks, gates, ups):
        grad_inner = jnp.einsum("td,fd->tf", block, full_down, preferred_element_type=jnp.float32)
        sigmoid_gate = jax.nn.sigmoid(gate_proj)
        grad_gate_rows = (
            grad_inner * up_proj * sigmoid_gate * (1.0 + gate_proj * (1.0 - sigmoid_gate))
        ).astype(jnp.bfloat16)
        grad_up_rows = (grad_inner * gate_proj * sigmoid_gate).astype(jnp.bfloat16)
        grad_boths.append(jnp.concatenate([grad_gate_rows, grad_up_rows], axis=1))
        normed_parts.append(
            jnp.einsum(
                "tf,df->td", grad_boths[-1], full_gate_up, preferred_element_type=jnp.float32
            ).astype(jnp.bfloat16)
        )
    grad_ffn_all = jnp.concatenate(grad_blocks, axis=0)
    grad_both = jnp.concatenate(grad_boths, axis=0)
    grad_normed = total_of(exchange(normed_parts)) + grad_two
    down_grad = jnp.einsum(
        "tf,td->fd", inner_act, grad_ffn_all, preferred_element_type=jnp.float32
    ).astype(jnp.bfloat16)
    both_grad = jnp.einsum(
        "td,tf->df", normed_all, grad_both, preferred_element_type=jnp.float32
    ).astype(jnp.bfloat16)
    ffn_grad = lax.psum_scatter(
        jnp.concatenate([both_grad, down_grad], axis=1),
        "fsdp",
        scatter_dimension=0,
        tiled=True,
    )

    grad_one, gain_one_grad, bias_one_grad = norm_back(
        grad_normed, normal_one, inverse_one, gain_first
    )
    grad_attn = grad_one.astype(jnp.bfloat16)
    grad_mix = jnp.einsum(
        "te,de->td", grad_attn, full_out, preferred_element_type=jnp.float32
    ).astype(jnp.bfloat16)
    leaving = [grad_mix[:, m * head_width : (m + 1) * head_width] for m in range(parts)]
    grad_heads = jnp.concatenate(exchange(leaving), axis=0)
    lead = max(1, heads - 1)
    back_args = (info, qkv_rows, head_out, grad_heads, log_rows, turns, heads)
    first_part = attend_back(*back_args, tuple(range(lead)), ())
    head_late, first_part = lax.optimization_barrier((head_mix, first_part))
    out_part = jnp.einsum(
        "td,te->de", head_late, grad_attn, preferred_element_type=jnp.float32
    ).astype(jnp.bfloat16)
    if shards <= direct_limit:
        out_part = regroup(out_part.reshape(parts, head_width, width), block_order, parts, head_width)
    else:
        out_part = jnp.take(out_part.reshape(parts, head_width, width), block_order, axis=0)
    vectors_part = (
        jnp.stack([gain_one_grad, bias_one_grad, gain_two_grad, bias_two_grad])
        .reshape(4, shards, shard_rows)
        .transpose(1, 0, 2)
        .reshape(shards, 1, 4 * shard_rows)
    )
    vectors_part = jnp.pad(vectors_part, ((0, 0), (0, 0), (0, width - 4 * shard_rows)))
    squares = jnp.stack(
        [
            jnp.sum(column * stream_float * stream_float, axis=0),
            jnp.sum(column * branch_attn * branch_attn, axis=0),
            jnp.sum(column * branch_ffn * branch_ffn, axis=0),
        ]
    )
    squares = jnp.broadcast_to(squares[None], (shards, 3, width))
    extra_part = jnp.concatenate(
        [vectors_part, squares, jnp.zeros((shards, 12, width), jnp.float32)], axis=1
    ).astype(jnp.bfloat16)
    out_part = jnp.concatenate([out_part.reshape(shards, shard_rows, width), extra_part], axis=1)
    out_part, first_part = lax.optimization_barrier((out_part, first_part))
    out_grad = lax.psum_scatter(
        out_part,
        "fsdp",
        scatter_dimension=0,
        tiled=True,
    )[0]
    out_blocks = [block.astype(jnp.float32) for block in spread(out_grad)]
    while len(out_blocks) > 1:
        out_blocks = [
            out_blocks[i] + out_blocks[i + 1] for i in range(0, len(out_blocks), 2)
        ]
    out_out = out_blocks[0][:shard_rows]
    vector_grads = out_blocks[0][shard_rows, : 4 * shard_rows].reshape(4, shard_rows)
    denominator = jnp.sum(seq_lens).astype(jnp.float32) * width
    stream_rms = jnp.sqrt(
        jnp.sum(out_blocks[0][shard_rows + 1 : shard_rows + 4], axis=1) / denominator
    )
    grad_proj = attend_back(*back_args, tuple(range(lead, heads)), (first_part,))
    token_parts = [
        jnp.einsum(
            "tc,dc->td",
            grad_proj[m * rows : (m + 1) * rows],
            full_qkv,
            preferred_element_type=jnp.float32,
        ).astype(jnp.bfloat16)
        for m in range(parts)
    ]
    arrived = exchange(token_parts)
    qkv_grad = scatter_rows(
        jnp.einsum("td,tc->dc", stream_all, grad_proj, preferred_element_type=jnp.float32).astype(
            jnp.bfloat16
        ),
    )
    qkv_low = qkv_grad.astype(jnp.bfloat16)
    grad_late = lax.optimization_barrier((grad_one, qkv_low, out_grad))[0]
    grad_tokens = (total_of(arrived) + grad_late).astype(jnp.bfloat16)
    qkv_blocks = unmix(spread(qkv_low), rank).astype(jnp.float32)
    qkv_out = (
        qkv_blocks.reshape(parts, shard_rows, 3, head_width)
        .transpose(1, 2, 0, 3)
        .reshape(shard_rows, 3 * width)
    )
    ffn_blocks = spread(ffn_grad.astype(jnp.bfloat16))
    if shards <= direct_limit:
        gate_out, up_out, down_out = restore(info, ffn_blocks, shards, piece)
    else:
        ffn_rows = unmix(ffn_blocks, rank).astype(jnp.float32)

        def widen(blocks):
            return (
                blocks.reshape(parts, shard_rows, shards, piece)
                .transpose(1, 2, 0, 3)
                .reshape(shard_rows, shards * hidden)
            )

        gate_out = widen(ffn_rows[:, :, :wide])
        up_out = widen(ffn_rows[:, :, wide : 2 * wide])
        down_out = ffn_rows[:, :, 2 * wide :].reshape(hidden, width)
    return (
        layer_out[None],
        grad_tokens[None],
        qkv_out,
        out_out,
        gate_out,
        up_out,
        down_out,
        vector_grads[0],
        vector_grads[1],
        vector_grads[2],
        vector_grads[3],
        stream_rms,
    )


def solution(mesh):
    placed = (
        P("fsdp", "seq", None),
        P("fsdp", "seq", None),
        P("fsdp", None),
        P("fsdp", None),
        P("fsdp", None),
        P("fsdp", None),
        P("fsdp", None),
        P("fsdp"),
        P("fsdp"),
        P("fsdp"),
        P("fsdp"),
        P(),
        P(),
    )

    return jax.shard_map(
        body,
        mesh=mesh,
        in_specs=placed,
        out_specs=(
            P("fsdp", "seq", None),
            P("fsdp", "seq", None),
            P("fsdp", None),
            P("fsdp", None),
            P("fsdp", None),
            P("fsdp", None),
            P("fsdp", None),
            P("fsdp"),
            P("fsdp"),
            P("fsdp"),
            P("fsdp"),
            P(),
        ),
        check_vma=False,
    )
```

```python
import functools

import jax
import jax.numpy as jnp
from jax import lax
from jax.experimental import pallas as pl
from jax.experimental.pallas import tpu as pltpu
from jax.sharding import PartitionSpec as P


HD = 64


epsilon = 1e-12
rope_base = 1000.0
direct_limit = 8


def rope_tables(positions, head_size):
    half_size = head_size // 2
    exponent = jnp.arange(half_size, dtype=jnp.float32) * (2.0 / head_size)
    frequency = jnp.power(jnp.float32(rope_base), -exponent)
    angles = positions[:, None] * frequency[None, :]
    cos_half = jnp.cos(angles)
    sin_half = jnp.sin(angles)
    return (
        jnp.concatenate([cos_half, cos_half], axis=-1),
        jnp.concatenate([sin_half, sin_half], axis=-1),
    )


def rotate(values_in, cos_table, sin_table):
    half_size = values_in.shape[-1] // 2
    turned = jnp.concatenate([-values_in[..., half_size:], values_in[..., :half_size]], axis=-1)
    return values_in * cos_table + turned * sin_table


def lookup(table, position):
    marks = jnp.arange(table.shape[0], dtype=jnp.int32) == position
    return jnp.sum(jnp.where(marks, table, 0))


def layer_norm(stream, gain_vec, bias_vec):
    average = jnp.mean(stream, axis=-1, keepdims=True)
    centred = stream - average
    variance = jnp.mean(centred * centred, axis=-1, keepdims=True)
    inverse = lax.rsqrt(variance + epsilon)
    normal = centred * inverse
    return (normal * gain_vec + bias_vec, normal, inverse)


def norm_back(grad_rows, normal, inverse, gain_vec):
    scaled = grad_rows * gain_vec
    first_mean = jnp.mean(scaled, axis=-1, keepdims=True)
    second_mean = jnp.mean(scaled * normal, axis=-1, keepdims=True)
    grad_in = (scaled - first_mean - normal * second_mean) * inverse
    return (grad_in, jnp.sum(grad_rows * normal, axis=0), jnp.sum(grad_rows, axis=0))


def flip(array, axis, mask):
    count = lax.axis_size(axis)
    return lax.ppermute(array, axis, [(i, i ^ mask) for i in range(count)])


def spread(block):
    return [block] + [flip(block, "seq", m) for m in range(1, lax.axis_size("seq"))]


def exchange(blocks):
    return [blocks[0]] + [flip(blocks[m], "seq", m) for m in range(1, len(blocks))]


def unmix(blocks, rank):
    stacked = jnp.stack(blocks)
    for m, block in enumerate(blocks):
        stacked = lax.dynamic_update_index_in_dim(stacked, block, rank ^ m, 0)
    return stacked


def place_kernel(count, order, *refs):
    out, sems = refs[count], refs[count + 1]
    copies = [
        pltpu.make_async_copy(refs[k], out.at[order[k]], sems.at[k]) for k in range(count)
    ]
    for copy in copies:
        copy.start()
    for copy in copies:
        copy.wait()


def place(blocks, order):
    count = len(blocks)
    shape = blocks[0].shape
    return pl.pallas_call(
        functools.partial(place_kernel, count),
        out_shape=jax.ShapeDtypeStruct((count,) + shape, blocks[0].dtype),
        in_specs=[pl.BlockSpec(memory_space=pltpu.SMEM)]
        + [pl.BlockSpec(memory_space=pl.ANY)] * count,
        out_specs=pl.BlockSpec(memory_space=pltpu.VMEM),
        scratch_shapes=[pltpu.SemaphoreType.DMA((count,))],
        name="place",
    )(order, *blocks)


def gather_rows(shard):
    count = lax.axis_size("fsdp")
    if count > direct_limit:
        return lax.all_gather(shard, "fsdp", axis=0, tiled=False)
    planes = count // 2
    owner = lax.axis_index("fsdp")
    plane = owner >> 1
    core = owner & 1
    blocks = [shard] + [
        lax.ppermute(shard, "fsdp", [(i, (i + 2 * k) % count) for i in range(count)])
        for k in range(1, planes)
    ]
    swapped = [flip(block, "fsdp", 1) for block in blocks]
    origin = 2 * ((plane - jnp.arange(planes, dtype=jnp.int32)) & (planes - 1))
    order = jnp.concatenate([origin + core, origin + 1 - core])
    return place(blocks + swapped, order)


def scatter_rows(grad):
    count = lax.axis_size("fsdp")
    if count > direct_limit:
        return lax.psum_scatter(grad, "fsdp", scatter_dimension=0, tiled=True).astype(jnp.float32)
    planes = count // 2
    owner = lax.axis_index("fsdp")
    plane = owner >> 1
    core = owner & 1
    view = grad.reshape(count, grad.shape[0] // count, grad.shape[1])

    def part(k, side):
        place_at = 2 * ((plane + k) & (planes - 1)) + (core ^ side)
        return lax.dynamic_index_in_dim(view, place_at, 0, keepdims=False)

    halves = {}
    for k in list(range(1, planes)) + [0]:
        halves[k] = part(k, 0).astype(jnp.float32) + flip(part(k, 1), "fsdp", 1).astype(jnp.float32)
    total = halves[0]
    for k in range(1, planes):
        total = total + lax.ppermute(
            halves[k].astype(jnp.bfloat16), "fsdp", [(i, (i + 2 * k) % count) for i in range(count)]
        ).astype(jnp.float32)
    return total


def regroup_kernel(groups, size, step, order, source, out, sems):
    per = source.shape[0] // groups
    copies = [
        pltpu.make_async_copy(
            source.at[f, :size],
            out.at[order[f // per], (f % per) * step : (f % per) * step + size],
            sems.at[f],
        )
        for f in range(source.shape[0])
    ]
    for copy in copies:
        copy.start()
    for copy in copies:
        copy.wait()


def regroup(source, order, groups, size):
    count, _, columns = source.shape
    return pl.pallas_call(
        functools.partial(regroup_kernel, groups, size, size),
        out_shape=jax.ShapeDtypeStruct((groups, count // groups * size, columns), source.dtype),
        in_specs=[
            pl.BlockSpec(memory_space=pltpu.SMEM),
            pl.BlockSpec(memory_space=pl.ANY),
        ],
        out_specs=pl.BlockSpec(memory_space=pltpu.VMEM),
        scratch_shapes=[pltpu.SemaphoreType.DMA((count,))],
        name="regroup",
    )(order, source)


def restore_kernel(parts, groups, piece, info, *refs):
    blocks, (gate, up, down), (held, sems) = refs[:parts], refs[parts : parts + 3], refs[parts + 3 :]
    wide = groups * piece
    rows = held.shape[1]
    copies = [
        pltpu.make_async_copy(blocks[m], held.at[info[0] ^ m], sems.at[m]) for m in range(parts)
    ]
    for copy in copies:
        copy.start()
    for copy in copies:
        copy.wait()
    for s in range(parts):
        down[s * rows : (s + 1) * rows, :] = held[s, :, 2 * wide :].astype(jnp.float32)
        for target, start in ((gate, 0), (up, wide)):
            for g in range(groups):
                target[:, (g * parts + s) * piece : (g * parts + s + 1) * piece] = held[
                    s, :, start + g * piece : start + (g + 1) * piece
                ].astype(jnp.float32)


def widen_kernel(parts, groups, piece, info, *refs):
    blocks, out, held, sems = refs[:parts], refs[parts], refs[parts + 1], refs[parts + 2]
    copies = [
        pltpu.make_async_copy(blocks[m], held.at[info[0] ^ m], sems.at[m]) for m in range(parts)
    ]
    for copy in copies:
        copy.start()
    for copy in copies:
        copy.wait()
    for s in range(parts):
        for g in range(groups):
            out[:, (g * parts + s) * piece : (g * parts + s + 1) * piece] = held[
                s, :, g * piece : (g + 1) * piece
            ].astype(jnp.float32)


def widen_blocks(info, blocks, groups, piece):
    parts = len(blocks)
    rows, total = blocks[0].shape
    return pl.pallas_call(
        functools.partial(widen_kernel, parts, groups, piece),
        out_shape=jax.ShapeDtypeStruct((rows, parts * total), jnp.float32),
        in_specs=[pl.BlockSpec(memory_space=pltpu.SMEM)]
        + [pl.BlockSpec(memory_space=pl.ANY)] * parts,
        out_specs=pl.BlockSpec(memory_space=pltpu.VMEM),
        scratch_shapes=[
            pltpu.VMEM((parts, rows, total), jnp.bfloat16),
            pltpu.SemaphoreType.DMA((parts,)),
        ],
        name="widen",
    )(info, *blocks)


def restore(info, blocks, groups, piece):
    parts = len(blocks)
    rows, total = blocks[0].shape
    wide = groups * piece
    whole = pl.BlockSpec(memory_space=pltpu.VMEM)
    return pl.pallas_call(
        functools.partial(restore_kernel, parts, groups, piece),
        out_shape=(
            jax.ShapeDtypeStruct((rows, parts * wide), jnp.float32),
            jax.ShapeDtypeStruct((rows, parts * wide), jnp.float32),
            jax.ShapeDtypeStruct((parts * rows, total - 2 * wide), jnp.float32),
        ),
        in_specs=[pl.BlockSpec(memory_space=pltpu.SMEM)]
        + [pl.BlockSpec(memory_space=pl.ANY)] * parts,
        out_specs=(whole, whole, whole),
        scratch_shapes=[
            pltpu.VMEM((parts, rows, total), jnp.bfloat16),
            pltpu.SemaphoreType.DMA((parts,)),
        ],
        name="restore",
    )(info, *blocks)


def total_of(blocks):
    out = blocks[0].astype(jnp.float32)
    for block in blocks[1:]:
        out = out + block.astype(jnp.float32)
    return out


tile = 256
log2e = 1.4426950408889634


def turn(left, right):
    return lax.dot_general(left, right, (((1,), (1,)), ((), ())), preferred_element_type=jnp.float32)


def times(left, right):
    return lax.dot_general(left, right, (((1,), (0,)), ((), ())), preferred_element_type=jnp.float32)


def valid_keys(info, key_tile, size):
    base = (info[0] ^ key_tile) * size
    return lax.broadcasted_iota(jnp.int32, (size, size), 0) < (info[1] - base)


def attend_kernel(heads, info, qkv, out, log_rows, scores):
    seqlen = qkv.shape[0]
    blocks = seqlen // tile
    width = heads * HD
    for h in range(heads):
        value_cols = qkv[:, 2 * width + h * HD : 2 * width + (h + 1) * HD]
        value_turned = value_cols.T

        def one_block(i, carry, h=h, value_turned=value_turned):
            rows = pl.ds(pl.multiple_of(i * tile, tile), tile)
            query = qkv[rows, h * HD : (h + 1) * HD]
            tops = None
            for j in range(blocks):
                keys = qkv[j * tile : (j + 1) * tile, width + h * HD : width + (h + 1) * HD]
                part = jnp.where(valid_keys(info, j, tile), turn(keys, query), -1e30)
                scores[j * tile : (j + 1) * tile, :] = part
                top = jnp.max(part, axis=0, keepdims=True)
                tops = top if tops is None else jnp.maximum(tops, top)
            mixed = None
            total = None
            for j in range(blocks):
                raised = jnp.exp2(
                    (scores[j * tile : (j + 1) * tile, :] - tops) * (log2e * HD ** (-0.5))
                )
                part = jnp.sum(raised, axis=0, keepdims=True)
                total = part if total is None else total + part
                piece = times(
                    value_turned[:, j * tile : (j + 1) * tile], raised.astype(jnp.bfloat16)
                )
                mixed = piece if mixed is None else mixed + piece
            out[rows, h * HD : (h + 1) * HD] = (mixed / total).T.astype(jnp.bfloat16)
            log_rows[h : h + 1, rows] = tops * (log2e * HD ** (-0.5)) + jnp.log2(total)
            return carry

        lax.fori_loop(0, blocks, one_block, 0)


def unturn(turned, turns):
    half = HD // 2
    cos, sin = turns[:half], turns[half:]
    first, second = turned[:half], turned[half:]
    return jnp.concatenate([first * cos + second * sin, second * cos - first * sin], axis=0)


def attend_back_kernel(heads, chosen, info, qkv, mixed, grads, log_rows, turns, *refs):
    out, key_sum, value_sum = refs[-3:]
    seqlen = qkv.shape[0]
    blocks = seqlen // tile
    width = heads * HD
    scale = HD ** (-0.5)
    step = out.shape[1] // 3
    shift = chosen[0] if step < width else 0
    if len(refs) > 3:
        known = refs[0].shape[1] // 3
        for part in range(3):
            out[:, part * step : part * step + known] = refs[0][
                :, part * known : (part + 1) * known
            ]
    for h in chosen:
        low, high = h * HD, (h + 1) * HD
        left, right = low - shift * HD, high - shift * HD
        key_turned = qkv[:, width + low : width + high].T
        key_sum[...] = jnp.zeros_like(key_sum)
        value_sum[...] = jnp.zeros_like(value_sum)

        def one_block(i, carry, low=low, high=high, h=h, left=left, right=right, key_turned=key_turned):
            rows = pl.ds(pl.multiple_of(i * tile, tile), tile)
            query = qkv[rows, low:high]
            grad = grads[rows, low:high]
            row_dot = jnp.sum(
                (grad.astype(jnp.float32) * mixed[rows, low:high].astype(jnp.float32)).T,
                axis=0,
                keepdims=True,
            )
            logs = log_rows[h : h + 1, rows]
            query_grad = None
            for j in range(blocks):
                span = slice(j * tile, (j + 1) * tile)
                keys = qkv[span, width + low : width + high]
                values = qkv[span, 2 * width + low : 2 * width + high]
                probs = jnp.where(
                    valid_keys(info, j, tile),
                    jnp.exp2(turn(keys, query) * (log2e * HD ** (-0.5)) - logs),
                    0.0,
                )
                grad_scores = (probs * (turn(values, grad) - row_dot)).astype(jnp.bfloat16)
                value_sum[span, :] += times(probs.astype(jnp.bfloat16), grad)
                key_sum[span, :] += times(grad_scores, query)
                piece = times(key_turned[:, span], grad_scores)
                query_grad = piece if query_grad is None else query_grad + piece
            out[rows, left:right] = unturn(query_grad * scale, turns[:, rows]).T.astype(jnp.bfloat16)
            return carry

        lax.fori_loop(0, blocks, one_block, 0)
        key_grad = unturn((key_sum[...] * scale).T, turns[...]).T
        out[:, step + left : step + right] = key_grad.astype(jnp.bfloat16)
        out[:, 2 * step + left : 2 * step + right] = value_sum[...].astype(jnp.bfloat16)


def attend(info, qkv, heads):
    seqlen = qkv.shape[0]
    whole = pl.BlockSpec(memory_space=pltpu.VMEM)
    return pl.pallas_call(
        functools.partial(attend_kernel, heads),
        out_shape=(
            jax.ShapeDtypeStruct((seqlen, heads * HD), jnp.bfloat16),
            jax.ShapeDtypeStruct((8, seqlen), jnp.float32),
        ),
        in_specs=[pl.BlockSpec(memory_space=pltpu.SMEM), whole],
        out_specs=(whole, whole),
        scratch_shapes=[pltpu.VMEM((seqlen, tile), jnp.float32)],
        cost_estimate=pl.CostEstimate(
            flops=16 * heads * seqlen * seqlen * HD, bytes_accessed=8 * seqlen * heads * HD,
            transcendentals=heads * seqlen * seqlen,
        ),
        name="attend",
    )(info, qkv)


def attend_back(info, qkv, mixed, grads, log_rows, turns, heads, chosen, known):
    seqlen = qkv.shape[0]
    whole = pl.BlockSpec(memory_space=pltpu.VMEM)
    count = heads if known else len(chosen)
    return pl.pallas_call(
        functools.partial(attend_back_kernel, heads, chosen),
        out_shape=jax.ShapeDtypeStruct((seqlen, 3 * count * HD), jnp.bfloat16),
        in_specs=[pl.BlockSpec(memory_space=pltpu.SMEM)] + [whole] * (5 + len(known)),
        out_specs=whole,
        scratch_shapes=[
            pltpu.VMEM((seqlen, HD), jnp.float32),
            pltpu.VMEM((seqlen, HD), jnp.float32),
        ],
        cost_estimate=pl.CostEstimate(
            flops=40 * len(chosen) * seqlen * seqlen * HD,
            bytes_accessed=16 * seqlen * heads * HD,
            transcendentals=len(chosen) * seqlen * seqlen,
        ),
    )(info, qkv, mixed, grads, log_rows, turns, *known)


def body(
    tokens,
    cotangent,
    w_qkv,
    w_out,
    w_gate,
    w_up,
    w_down,
    gain_one,
    bias_one,
    gain_two,
    bias_two,
    seq_lens,
    slot_seq,
):
    parts = lax.axis_size("seq")
    shards = lax.axis_size("fsdp")
    rank = lax.axis_index("seq")
    owner = lax.axis_index("fsdp")
    rows = tokens.shape[1]
    width = tokens.shape[2]
    shard_rows = w_qkv.shape[0]
    heads = width // HD // parts
    head_width = heads * HD
    hidden = w_down.shape[0]
    piece = hidden // parts
    wide = shards * piece
    seqlen = rows * parts
    stream_in = tokens[0]
    length = lookup(seq_lens, lookup(slot_seq, owner))
    own = jnp.arange(rows, dtype=jnp.int32)
    positions = rank * rows + own
    column = (positions < length).astype(jnp.float32)[:, None]
    block_order = jnp.arange(parts, dtype=jnp.int32) ^ rank
    all_positions = (block_order[:, None] * rows + own[None, :]).reshape(seqlen)
    info = jnp.stack([rank.astype(jnp.int32), length.astype(jnp.int32)])

    stream_blocks = spread(stream_in)
    qkv_piece = lax.dynamic_index_in_dim(
        w_qkv.reshape(shard_rows, 3, parts, head_width), rank, 2, keepdims=False
    ).reshape(shard_rows, 3 * head_width)
    full_qkv = gather_rows(qkv_piece).reshape(width, 3 * head_width)

    def columns_of(weight):
        return lax.dynamic_index_in_dim(
            weight.reshape(shard_rows, shards, parts, piece), rank, 2, keepdims=False
        ).reshape(shard_rows, wide)

    vectors = jnp.concatenate([gain_one, bias_one, gain_two, bias_two])
    vectors = jnp.pad(vectors, (0, width - vectors.shape[0])).reshape(1, width)
    out_piece = jnp.concatenate([w_out, jnp.pad(vectors, ((0, 15), (0, 0)))], axis=0)
    down_piece = lax.dynamic_slice_in_dim(w_down, rank * piece, piece, 0)
    ffn_piece = jnp.concatenate(
        [
            columns_of(w_gate),
            columns_of(w_up),
            down_piece,
        ],
        axis=1,
    )
    gathered_out = lax.all_gather(out_piece, "fsdp", axis=0, tiled=False)
    if shards <= direct_limit:
        full_out = regroup(gathered_out, block_order, parts, shard_rows).reshape(width, width)
    else:
        full_out = jnp.take(
            gathered_out[:, :shard_rows].reshape(parts, head_width, width), block_order, axis=0
        ).reshape(width, width)
    params = gathered_out[:, shard_rows, : 4 * shard_rows].astype(jnp.float32)
    params = params.reshape(shards, 4, shard_rows).transpose(1, 0, 2).reshape(4, width)
    gain_first, bias_first, gain_second, bias_second = (params[i : i + 1] for i in range(4))
    full_ffn = lax.all_gather(ffn_piece, "fsdp", axis=0, tiled=True)
    full_gate_up = full_ffn[:, : 2 * wide]
    full_down = full_ffn[:, 2 * wide :]

    stream_all = jnp.concatenate(stream_blocks, axis=0)
    projected = jnp.dot(stream_all, full_qkv, preferred_element_type=jnp.float32).reshape(
        seqlen, 3, heads, HD
    )
    cos_table, sin_table = rope_tables(all_positions.astype(jnp.float32), HD)
    turns = jnp.concatenate([cos_table[:, : HD // 2].T, sin_table[:, : HD // 2].T], axis=0)
    cos_table = cos_table[:, None, :]
    sin_table = sin_table[:, None, :]
    queries = rotate(projected[:, 0], cos_table, sin_table).astype(jnp.bfloat16)
    key_rows = rotate(projected[:, 1], cos_table, sin_table).astype(jnp.bfloat16)
    values = projected[:, 2].astype(jnp.bfloat16)
    qkv_rows = jnp.stack([queries, key_rows, values], axis=1).reshape(seqlen, 3 * head_width)
    head_out, log_rows = attend(info, qkv_rows, heads)
    mixed = exchange([head_out[m * rows : (m + 1) * rows] for m in range(parts)])
    head_mix = jnp.concatenate(mixed, axis=1)
    branch_attn = jnp.dot(head_mix, full_out, preferred_element_type=jnp.float32)
    stream_float = stream_in.astype(jnp.float32)
    normed_float, normal_one, inverse_one = layer_norm(
        stream_float + branch_attn, gain_first, bias_first
    )
    normed_one = normed_float.astype(jnp.bfloat16)
    normed_blocks = spread(normed_one)
    gates, ups, inners, ffn_parts = [], [], [], []
    for block in normed_blocks:
        gate_up = jnp.dot(block, full_gate_up, preferred_element_type=jnp.float32)
        gates.append(gate_up[:, :wide])
        ups.append(gate_up[:, wide:])
        inners.append((jax.nn.silu(gates[-1]) * ups[-1]).astype(jnp.bfloat16))
        ffn_parts.append(
            jnp.dot(inners[-1], full_down, preferred_element_type=jnp.float32).astype(jnp.bfloat16)
        )
    normed_all = jnp.concatenate(normed_blocks, axis=0)
    inner_act = jnp.concatenate(inners, axis=0)
    branch_ffn = total_of(exchange(ffn_parts))
    out_float, normal_two, inverse_two = layer_norm(
        normed_one.astype(jnp.float32) + branch_ffn, gain_second, bias_second
    )
    layer_out = (out_float * column).astype(jnp.bfloat16)
    grad_rows = cotangent[0].astype(jnp.float32) * column
    grad_two, gain_two_grad, bias_two_grad = norm_back(
        grad_rows, normal_two, inverse_two, gain_second
    )
    grad_ffn = grad_two.astype(jnp.bfloat16)
    grad_blocks = spread(grad_ffn)
    grad_boths, normed_parts = [], []
    for block, gate_proj, up_proj in zip(grad_blocks, gates, ups):
        grad_inner = jnp.einsum("td,fd->tf", block, full_down, preferred_element_type=jnp.float32)
        sigmoid_gate = jax.nn.sigmoid(gate_proj)
        grad_gate_rows = (
            grad_inner * up_proj * sigmoid_gate * (1.0 + gate_proj * (1.0 - sigmoid_gate))
        ).astype(jnp.bfloat16)
        grad_up_rows = (grad_inner * gate_proj * sigmoid_gate).astype(jnp.bfloat16)
        grad_boths.append(jnp.concatenate([grad_gate_rows, grad_up_rows], axis=1))
        normed_parts.append(
            jnp.einsum(
                "tf,df->td", grad_boths[-1], full_gate_up, preferred_element_type=jnp.float32
            ).astype(jnp.bfloat16)
        )
    grad_ffn_all = jnp.concatenate(grad_blocks, axis=0)
    grad_both = jnp.concatenate(grad_boths, axis=0)
    grad_normed = total_of(exchange(normed_parts)) + grad_two
    down_grad = jnp.einsum(
        "tf,td->fd", inner_act, grad_ffn_all, preferred_element_type=jnp.float32
    ).astype(jnp.bfloat16)
    both_grad = jnp.einsum(
        "td,tf->df", normed_all, grad_both, preferred_element_type=jnp.float32
    ).astype(jnp.bfloat16)
    ffn_grad = lax.psum_scatter(
        jnp.concatenate([both_grad, down_grad], axis=1),
        "fsdp",
        scatter_dimension=0,
        tiled=True,
    )

    grad_one, gain_one_grad, bias_one_grad = norm_back(
        grad_normed, normal_one, inverse_one, gain_first
    )
    grad_attn = grad_one.astype(jnp.bfloat16)
    grad_mix = jnp.einsum(
        "te,de->td", grad_attn, full_out, preferred_element_type=jnp.float32
    ).astype(jnp.bfloat16)
    leaving = [grad_mix[:, m * head_width : (m + 1) * head_width] for m in range(parts)]
    grad_heads = jnp.concatenate(exchange(leaving), axis=0)
    lead = max(1, heads - 1)
    back_args = (info, qkv_rows, head_out, grad_heads, log_rows, turns, heads)
    first_part = attend_back(*back_args, tuple(range(lead)), ())
    head_late, first_part = lax.optimization_barrier((head_mix, first_part))
    out_part = jnp.einsum(
        "td,te->de", head_late, grad_attn, preferred_element_type=jnp.float32
    ).astype(jnp.bfloat16)
    if shards <= direct_limit:
        out_part = regroup(out_part.reshape(parts, head_width, width), block_order, parts, head_width)
    else:
        out_part = jnp.take(out_part.reshape(parts, head_width, width), block_order, axis=0)
    vectors_part = (
        jnp.stack([gain_one_grad, bias_one_grad, gain_two_grad, bias_two_grad])
        .reshape(4, shards, shard_rows)
        .transpose(1, 0, 2)
        .reshape(shards, 1, 4 * shard_rows)
    )
    vectors_part = jnp.pad(vectors_part, ((0, 0), (0, 0), (0, width - 4 * shard_rows)))
    squares = jnp.stack(
        [
            jnp.sum(column * stream_float * stream_float, axis=0),
            jnp.sum(column * branch_attn * branch_attn, axis=0),
            jnp.sum(column * branch_ffn * branch_ffn, axis=0),
        ]
    )
    squares = jnp.broadcast_to(squares[None], (shards, 3, width))
    extra_part = jnp.concatenate(
        [vectors_part, squares, jnp.zeros((shards, 12, width), jnp.float32)], axis=1
    ).astype(jnp.bfloat16)
    out_part = jnp.concatenate([out_part.reshape(shards, shard_rows, width), extra_part], axis=1)
    out_part, first_part = lax.optimization_barrier((out_part, first_part))
    out_grad = lax.psum_scatter(
        out_part,
        "fsdp",
        scatter_dimension=0,
        tiled=True,
    )[0]
    out_blocks = [block.astype(jnp.float32) for block in spread(out_grad)]
    while len(out_blocks) > 1:
        out_blocks = [
            out_blocks[i] + out_blocks[i + 1] for i in range(0, len(out_blocks), 2)
        ]
    out_out = out_blocks[0][:shard_rows]
    vector_grads = out_blocks[0][shard_rows, : 4 * shard_rows].reshape(4, shard_rows)
    denominator = jnp.sum(seq_lens).astype(jnp.float32) * width
    stream_rms = jnp.sqrt(
        jnp.sum(out_blocks[0][shard_rows + 1 : shard_rows + 4], axis=1) / denominator
    )
    grad_proj = attend_back(*back_args, tuple(range(lead, heads)), (first_part,))
    token_parts = [
        jnp.einsum(
            "tc,dc->td",
            grad_proj[m * rows : (m + 1) * rows],
            full_qkv,
            preferred_element_type=jnp.float32,
        ).astype(jnp.bfloat16)
        for m in range(parts)
    ]
    arrived = exchange(token_parts)
    qkv_grad = scatter_rows(
        jnp.einsum("td,tc->dc", stream_all, grad_proj, preferred_element_type=jnp.float32).astype(
            jnp.bfloat16
        ),
    )
    qkv_low = qkv_grad.astype(jnp.bfloat16)
    grad_late = lax.optimization_barrier((grad_one, qkv_low, out_grad))[0]
    grad_tokens = (total_of(arrived) + grad_late).astype(jnp.bfloat16)
    qkv_blocks = spread(qkv_low)
    if shards <= direct_limit:
        qkv_out = widen_blocks(info, qkv_blocks, 3, head_width)
    else:
        qkv_out = (
            unmix(qkv_blocks, rank)
            .astype(jnp.float32)
            .reshape(parts, shard_rows, 3, head_width)
            .transpose(1, 2, 0, 3)
            .reshape(shard_rows, 3 * width)
        )
    ffn_blocks = spread(ffn_grad.astype(jnp.bfloat16))
    if shards <= direct_limit:
        gate_out, up_out, down_out = restore(info, ffn_blocks, shards, piece)
    else:
        ffn_rows = unmix(ffn_blocks, rank).astype(jnp.float32)

        def widen(blocks):
            return (
                blocks.reshape(parts, shard_rows, shards, piece)
                .transpose(1, 2, 0, 3)
                .reshape(shard_rows, shards * hidden)
            )

        gate_out = widen(ffn_rows[:, :, :wide])
        up_out = widen(ffn_rows[:, :, wide : 2 * wide])
        down_out = ffn_rows[:, :, 2 * wide :].reshape(hidden, width)
    return (
        layer_out[None],
        grad_tokens[None],
        qkv_out,
        out_out,
        gate_out,
        up_out,
        down_out,
        vector_grads[0],
        vector_grads[1],
        vector_grads[2],
        vector_grads[3],
        stream_rms,
    )


def solution(mesh):
    placed = (
        P("fsdp", "seq", None),
        P("fsdp", "seq", None),
        P("fsdp", None),
        P("fsdp", None),
        P("fsdp", None),
        P("fsdp", None),
        P("fsdp", None),
        P("fsdp"),
        P("fsdp"),
        P("fsdp"),
        P("fsdp"),
        P(),
        P(),
    )

    return jax.shard_map(
        body,
        mesh=mesh,
        in_specs=placed,
        out_specs=(
            P("fsdp", "seq", None),
            P("fsdp", "seq", None),
            P("fsdp", None),
            P("fsdp", None),
            P("fsdp", None),
            P("fsdp", None),
            P("fsdp", None),
            P("fsdp"),
            P("fsdp"),
            P("fsdp"),
            P("fsdp"),
            P(),
        ),
        check_vma=False,
    )
```
